32 devices in a mesh: tm: 16 (over z, y, x), row: 2 (over core).
Axes of the slice: x: 2, y: 2, z: 4, core: 2. Of those that a mesh axis runs over, the one named last changes fastest.
Arguments:
- initial: float32 [1024], replicated, may hold values from -6 to 6
- dynamics: float32 [1024, 1024], replicated, may hold values from -0.009765625 to 0.009765625
- obs_rows: bfloat16 [32768, 1024], P('tm', 'row'), may hold values from -0.1875 to 0.1875
- obs_values: bfloat16 [32768], P('tm'), may hold values from -6 to 6
- obs_slab: int32 [32768, 1], P('tm'), may hold values from 0 to 31; in each aligned block of 2048 rows (0 to 2047, 2048 to 4095, ...) at most 64 rows name the same one
Outputs:
- states: float32 [32, 1024], P('tm', 'row')
The draws below stay inside these ranges and needn't reach their ends.
Inputs may be any that keep to these rules, and one draw needn't show every extreme that they name: `obs_slab`: within the rows ingested by one index of tm, no slab is named by more than 64 rows, a bound that some block reaches of them.
All inputs are finite; a program needn't handle non-finite values.
Results may differ from the reference program's by a relative error of at most 0.0003.
Values may be sent and summed in bfloat16 or wider, within the bound.
A program may use at most 128 MiB of HBM per device.

```python
import math
import jax
import jax.numpy as jnp
import numpy as np
from jax import lax

S = 1024
OBS_DEV = 2048
CAP = 64
SLABS = 32
OBS = 32768


def block_scale(key, extent, pieces, least, high):
    factor_of = 1.0
    for axis_at, blocks in pieces:
        heights = jax.random.uniform(jax.random.fold_in(jax.random.fold_in(key, 6), axis_at), (blocks,), jnp.float32, least / len(pieces), high / len(pieces))
        factor_of = factor_of * jnp.repeat(jnp.exp(heights), extent[axis_at] // blocks).reshape((-1,) + (1,) * (len(extent) - 1 - axis_at))
    return factor_of


def shared_out(rng, own, number, rows, count, top, reach, lean):
    ranking = jax.random.permutation(rng, count)
    crowded, usual = load_shares(count, rows * top, reach, lean, True), load_shares(count, rows * top, reach, lean, False)
    places = jnp.arange(count)

    def named(lengths, offset_by):
        used = int((lengths > 0).sum())
        fixed = max(1, used // 4)
        passed = fixed + (places - fixed + offset_by * (used - fixed)) % max(1, count - fixed)
        return jnp.zeros((count,), jnp.int32).at[ranking[jnp.where(places < fixed, places, passed)]].set(jnp.asarray(lengths, jnp.int32))

    lengths = jnp.where(number % 4 == 0, named(crowded, number // 4), named(usual, number - number // 4 - 1))
    mixed = jax.random.permutation(jax.random.fold_in(own, 3), count)
    giver, sink = mixed[0:count // 2 * 2:2], mixed[1:count // 2 * 2:2]
    margin = jnp.minimum(lengths[giver] - 1, reach - lengths[sink]) // 2
    margin = jnp.where((giver == ranking[0]) | (sink == ranking[0]) | (lengths[sink] == 0), 0, jnp.maximum(margin, 0))
    passed = jax.random.randint(jax.random.fold_in(own, 4), (count // 2,), 0, 1 << 20) % (margin + 1)
    lengths = lengths.at[giver].add(-passed).at[sink].add(passed)
    members = jnp.searchsorted(jnp.cumsum(lengths), jnp.arange(rows * top), side="right").astype(jnp.int32)
    grid = members.reshape(top, rows).T
    grid = grid[jax.random.permutation(jax.random.fold_in(own, 1), rows)]
    offset_by = jax.random.randint(jax.random.fold_in(own, 2), (rows, 1), 0, top)
    return jnp.take_along_axis(grid, (jnp.arange(top)[None, :] + offset_by) % top, axis=1)


def load_shares(amount, total, reach, lean, full):
    portions = [(1 << 20) // math.isqrt(rank ** lean) + 1 for rank in range(1, amount + 1)]
    largest = reach if full else min(reach, max(-(-total // amount), total * portions[0] // sum(portions)))
    least = 1 if total - largest >= amount - 1 else 0
    given, spare = [largest] + [least] * (amount - 1), total - largest - least * (amount - 1)
    while spare > 0:
        free = [i for i in range(1, amount) if given[i] < largest] or [i for i in range(1, amount) if given[i] < reach]
        pool, budget = sum([portions[i] for i in free]), spare
        for i in free:
            extra = min(reach - given[i], max(1, budget * portions[i] // pool), spare)
            given[i] = given[i] + extra
            spare = spare - extra
    return np.array(given)


def centred(own_key, shape, deviation, bound, pieces=(), held_as=jnp.bfloat16):
    array = jax.random.normal(own_key, shape, jnp.float32) * deviation
    if len(pieces) > 0:
        array = block_scale(own_key, shape, pieces, -0.22, 0.18) * array
    return jnp.clip(array, min=-bound, max=bound).astype(held_as)


def setup_inputs(seed: int = 0) -> dict:
    streams_of = jax.random.split(jax.random.key(seed), 6)
    initial = centred(streams_of[0], (S,), 1.0, 6.0, (), jnp.float32)
    dynamics = centred(streams_of[1], (S, S), (400 * S) ** -0.5, 0.009765625, (), jnp.float32)
    obs_rows = centred(streams_of[2], (OBS, S), S ** -0.5, 0.1875, ((0, 16), (1, 2)))
    obs_values = centred(streams_of[3], (OBS,), 1.0, 6.0, ((0, 16),))
    obs_slab_keys = jax.random.split(jax.random.fold_in(streams_of[4], 1), OBS // OBS_DEV)
    obs_slab_turns = jax.random.permutation(jax.random.fold_in(streams_of[4], 3), OBS // OBS_DEV)
    obs_slab = jax.vmap(lambda own, number: shared_out(jax.random.fold_in(streams_of[4], 2), own, number, OBS_DEV, SLABS, 1, CAP, 2))(obs_slab_keys, obs_slab_turns).reshape((OBS, 1))
    return dict(initial=initial, dynamics=dynamics, obs_rows=obs_rows, obs_values=obs_values, obs_slab=obs_slab)


def reference(initial, dynamics, obs_rows, obs_values, obs_slab):
    evolve = jnp.eye(S, dtype=jnp.float32) + dynamics
    rows_f32 = obs_rows.astype(jnp.float32)
    values_f32 = obs_values.astype(jnp.float32)
    target = obs_slab[:, 0]

    def advance(state, slab_index):
        moved = jnp.dot(evolve, state, precision=lax.Precision.HIGHEST)
        in_slab = (target == slab_index).astype(jnp.float32)
        misfit = in_slab * (values_f32 - jnp.dot(rows_f32, moved, precision=lax.Precision.HIGHEST))
        updated = moved + 0.3 * jnp.dot(misfit, rows_f32, precision=lax.Precision.HIGHEST)
        return updated, updated

    final_state, states = lax.scan(advance, initial, jnp.arange(SLABS, dtype=jnp.int32))
    return states
```

```python
import jax
import jax.numpy as jnp
from jax import lax
from jax.experimental import pallas as pl
from jax.experimental.pallas import tpu as pltpu
from jax.sharding import PartitionSpec as P

CAP = 64
LANES = 128
MESH = pl.DeviceIdType.MESH

sigma_gain = 0.3


def visit(own, turn, total):
    if total & (total - 1):
        return lax.rem(own + turn, total)
    if total == 4:
        turn = ((turn & 1) << 1) | (turn >> 1)
    return own ^ turn


def chip_at(place, planes):
    column = place // planes
    depth = lax.rem(place, planes)
    depth = jnp.where(column & 1 == 1, depth, planes - 1 - depth)
    turn = (column + 3) & 3
    return depth * 4 + (turn ^ (turn >> 1))


def place_of(chip, planes):
    depth, turn = chip // 4, chip & 3
    column = ((turn ^ (turn >> 1)) + 1) & 3
    depth = jnp.where(column & 1 == 1, depth, planes - 1 - depth)
    return column * planes + depth


def observer_kernel(
    target_ref, rows_ref, values_ref, dynamics_ref, start_ref, out_ref,
    sent, sent_values, slot_ref, got, got_values, dynamics, dyn_high, dyn_low, turned, gain, moment,
    high_ref, low_ref, b_ref, perm, high_got, low_got, b_got, came, went, back, offset,
    row_send, row_recv, value_send, value_recv, own_sem, send_sem, recv_sem, tile_send, tile_recv, out_send, out_recv,
):
    time_devs, row_devs = lax.axis_size("tm"), lax.axis_size("row")
    t, r = lax.axis_index("tm"), lax.axis_index("row")
    slabs = time_devs * row_devs
    last = time_devs - 1
    planes = time_devs // 4
    place_here = place_of(t, planes)
    after = chip_at(jnp.minimum(place_here + 1, last), planes)
    me = place_here * row_devs + r
    here = t * row_devs + r
    partner = (t, 1 - r)
    count, local = rows_ref.shape
    width = local * row_devs
    subs = width // LANES
    tile = 256
    tiles = width // tile
    block = 256
    share = block // CAP
    blocks = slabs // share

    def device(slab):
        return (chip_at(slab // row_devs, planes), lax.rem(slab, row_devs))

    barrier = pltpu.get_barrier_semaphore()

    def greet(slab, _):
        @pl.when(slab != me)
        def _():
            pl.semaphore_signal(barrier, inc=1, device_id=device(slab), device_id_type=MESH)

        return 0

    lax.fori_loop(0, slabs, greet, 0)
    fetch = pltpu.make_async_copy(dynamics_ref, dynamics, own_sem.at[2])
    fetch.start()

    before = (
        lax.broadcasted_iota(jnp.int32, (block, block), 0)
        < lax.broadcasted_iota(jnp.int32, (block, block), 1)
    ).astype(jnp.float32).astype(jnp.bfloat16)
    slab_of = lax.broadcasted_iota(jnp.int32, (slabs, block), 0)
    carry = (slab_of[:, :1] * CAP).astype(jnp.float32)
    for start in range(0, count, block):
        named = (target_ref[:, start : start + block] == slab_of).astype(jnp.float32)
        ahead = jnp.dot(named.astype(jnp.bfloat16), before, preferred_element_type=jnp.float32)
        slot = jnp.sum(named * (ahead + carry), axis=0, keepdims=True)
        slot_ref[:, start : start + block] = slot.astype(jnp.int32)
        carry = carry + jnp.sum(named, axis=1, keepdims=True)

    values = jnp.broadcast_to(values_ref[...].astype(jnp.float32), (8, count)).astype(jnp.bfloat16)
    sent_values[...] = jnp.zeros_like(sent_values)

    def landing(source):
        rows = pl.ds(pl.multiple_of(source // row_devs * CAP, CAP), CAP)
        cols = pl.ds(pl.multiple_of(lax.rem(source, row_devs) * local, local), local)
        return got.at[rows, cols]

    def copies(slab, source):
        rows = pltpu.make_async_remote_copy(
            src_ref=sent.at[slab], dst_ref=landing(source),
            send_sem=row_send.at[slab], recv_sem=row_recv.at[source],
            device_id=device(slab), device_id_type=MESH,
        )
        tags = pltpu.make_async_remote_copy(
            src_ref=sent_values.at[slab], dst_ref=got_values.at[source],
            send_sem=value_send.at[slab], recv_sem=value_recv.at[source],
            device_id=device(slab), device_id_type=MESH,
        )
        return rows, tags

    keep = (
        pltpu.make_async_copy(sent.at[me], landing(here), own_sem.at[0]),
        pltpu.make_async_copy(sent_values.at[me], got_values.at[here], own_sem.at[1]),
    )

    def place(at):
        first = at * share
        wanted = lax.broadcasted_iota(jnp.int32, (block, count), 0) + first * CAP
        pick = (wanted == slot_ref[...]).astype(jnp.float32).astype(jnp.bfloat16)
        rows = jnp.dot(pick, rows_ref[...], preferred_element_type=jnp.float32).astype(jnp.bfloat16)
        tags = lax.dot_general(
            values, pick, (((1,), (1,)), ((), ())), preferred_element_type=jnp.float32
        )[:1]
        for inner in range(share):
            sent[first + inner] = rows[inner * CAP : (inner + 1) * CAP]
            sent_values[first + inner, :, :CAP] = tags[:, inner * CAP : (inner + 1) * CAP]

    column_blocks = planes * row_devs // share
    depth = t // 4

    def order(turn):
        column = turn // column_blocks
        along = jnp.where(column & 1 == 1, depth, planes - 1 - depth)
        own = along * row_devs // share
        return column * column_blocks + (own ^ lax.rem(turn, column_blocks)), along

    def send(turn):
        at, along = order(turn)
        key = lax.rem(along * row_devs, share) + r
        for inner in range(share):
            slab = at * share + (key ^ inner)

            @pl.when(slab != me)
            def _():
                for copy in copies(slab, here):
                    copy.start()

            @pl.when(slab == me)
            def _():
                for copy in keep:
                    copy.start()

    place(order(0)[0])
    pl.semaphore_wait(barrier, slabs - 1)
    send(0)

    def step(turn, _):
        place(order(turn)[0])
        send(turn)
        return 0

    lax.fori_loop(1, blocks, step, 0)

    fetch.wait()

    def divide(k, _):
        rows = pl.ds(pl.multiple_of(k * LANES, LANES), LANES)
        high = dynamics[rows, :].astype(jnp.bfloat16)
        dyn_high[rows, :] = high
        dyn_low[rows, :] = (dynamics[rows, :] - high.astype(jnp.float32)).astype(jnp.bfloat16)
        return 0

    lax.fori_loop(0, subs, divide, 0)
    gain[...] = jnp.zeros_like(gain)
    moment[...] = jnp.zeros_like(moment)

    chips = block // CAP
    groups = time_devs // chips
    nearest = t // chips

    def gather(turn, _):
        at = visit(nearest, turn, groups)

        def arrive(source, _):
            @pl.when(source != here)
            def _():
                for copy in copies(me, source):
                    copy.wait_recv()

            @pl.when(source == here)
            def _():
                for copy in keep:
                    copy.wait()

            return 0

        lax.fori_loop(at * chips * row_devs, (at + 1) * chips * row_devs, arrive, 0)
        own = pl.ds(pl.multiple_of(at * block, block), block)
        rows = got[own, :]
        turned[...] = rows.T
        tags = jnp.concatenate(
            [got_values[(at * chips + k) * row_devs][:, :CAP] for k in range(chips)], axis=1
        )
        tags = jnp.broadcast_to(tags, (8, block)).astype(jnp.bfloat16)
        moment[...] += jnp.dot(tags, rows, preferred_element_type=jnp.float32)

        def column(k, _):
            cols = pl.ds(pl.multiple_of(k * tile, tile), tile)
            seen = (
                got[own, cols].astype(jnp.float32)
                + jnp.dot(got[own, :], dyn_high[:, cols], preferred_element_type=jnp.float32)
                + jnp.dot(got[own, :], dyn_low[:, cols], preferred_element_type=jnp.float32)
            )
            high = seen.astype(jnp.bfloat16)
            low = (seen - high.astype(jnp.float32)).astype(jnp.bfloat16)
            gain[:, cols] += jnp.dot(
                turned[...], high, preferred_element_type=jnp.float32
            ) + jnp.dot(turned[...], low, preferred_element_type=jnp.float32)
            return 0

        lax.fori_loop(0, tiles, column, 0)
        return 0

    lax.fori_loop(0, groups, gather, 0)

    def push(source, target, index, peer):
        return pltpu.make_async_remote_copy(
            src_ref=source, dst_ref=target, send_sem=send_sem.at[index],
            recv_sem=recv_sem.at[index], device_id=peer, device_id_type=MESH,
        )

    lend = push(b_ref, b_got, 0, partner)
    onward = push(went, came, 2, (after, 1))
    aside = pltpu.make_async_remote_copy(
        src_ref=went, dst_ref=came, send_sem=send_sem.at[3],
        recv_sem=recv_sem.at[2], device_id=(after, 0), device_id_type=MESH,
    )

    def part(k):
        cols = pl.ds(pl.multiple_of(k * tile, tile), tile)
        return [
            pltpu.make_async_remote_copy(
                src_ref=source.at[:, cols], dst_ref=target.at[:, cols],
                send_sem=tile_send.at[index, k], recv_sem=tile_recv.at[index, k],
                device_id=partner, device_id_type=MESH,
            )
            for index, (source, target) in enumerate(((high_ref, high_got), (low_ref, low_got)))
        ]

    for sub in range(subs):
        b_ref[sub : sub + 1, :] = sigma_gain * moment[:1, sub * LANES : (sub + 1) * LANES]

    @pl.when(r == 0)
    def _():
        lend.start()

    def settle(k, _):
        cols = pl.ds(pl.multiple_of(k * tile, tile), tile)
        for sub in range(subs):
            own = slice(sub * LANES, (sub + 1) * LANES)
            diagonal = (
                lax.broadcasted_iota(jnp.int32, (LANES, tile), 0) + sub * LANES
                == lax.broadcasted_iota(jnp.int32, (LANES, tile), 1) + k * tile
            ).astype(jnp.float32)
            whole = diagonal + dynamics[own, cols] - sigma_gain * gain[own, cols]
            high = whole.astype(jnp.bfloat16)
            high_ref[own, cols] = high
            low_ref[own, cols] = (whole - high.astype(jnp.float32)).astype(jnp.bfloat16)
            perm[:, sub, cols] = whole

        @pl.when(r == 0)
        def _():
            for copy in part(k):
                copy.start()

        return 0

    lax.fori_loop(0, tiles, settle, 0)

    lane = lax.broadcasted_iota(jnp.int32, (subs, LANES), 1)
    group = 16

    def apply(vector):
        pieces = [jnp.broadcast_to(vector[k : k + 1, :], (subs, LANES)) for k in range(subs)]

        def rows(step, total):
            for inner in range(group):
                g = step * group + inner
                part = perm[g, :, 0:LANES] * pieces[0]
                for k in range(1, subs):
                    part = part + perm[g, :, k * LANES : (k + 1) * LANES] * pieces[k]
                total = jnp.where(lane == g, jnp.sum(part, axis=1, keepdims=True), total)
            return total

        return lax.fori_loop(0, LANES // group, rows, jnp.zeros((subs, LANES), jnp.float32))

    offset[...] = b_ref[...]

    @pl.when(r == 1)
    def _():
        lend.wait_recv()
        offset[...] = apply(b_got[...]) + b_ref[...]

        def compose(k, _):
            for copy in part(k):
                copy.wait_recv()
            cols = pl.ds(pl.multiple_of(k * tile, tile), tile)
            high, low = high_got[:, cols], low_got[:, cols]
            whole = (
                jnp.dot(high_ref[...], high, preferred_element_type=jnp.float32)
                + jnp.dot(high_ref[...], low, preferred_element_type=jnp.float32)
                + jnp.dot(low_ref[...], high, preferred_element_type=jnp.float32)
            )
            for sub in range(subs):
                perm[:, sub, cols] = whole[sub * LANES : (sub + 1) * LANES, :]
            return 0

        lax.fori_loop(0, tiles, compose, 0)

    @pl.when(r == 0)
    def _():
        lend.wait_send()

        def drain(k, _):
            for copy in part(k):
                copy.wait_send()
            return 0

        lax.fori_loop(0, tiles, drain, 0)

    @pl.when(place_here == 0)
    def _():
        came[...] = start_ref[...]

    @pl.when(place_here > 0)
    def _():
        onward.wait_recv()

    went[...] = apply(came[...]) + offset[...]
    passing = (r == 1) & (place_here < last)

    @pl.when(passing)
    def _():
        onward.start()
        aside.start()

    stays = place_here == t

    def report(core, sender):
        return pltpu.make_async_remote_copy(
            src_ref=went, dst_ref=back.at[sender], send_sem=out_send.at[core],
            recv_sem=out_recv.at[sender], device_id=(place_here, core), device_id_type=MESH,
        )

    for core in range(2):
        @pl.when(jnp.logical_not(stays & (r == core)))
        def _():
            report(core, r).start()

        @pl.when(stays & (r == core))
        def _():
            back[core] = went[...]

    for core in range(2):
        @pl.when(jnp.logical_not(stays & (r == core)))
        def _():
            report(core, core).wait_recv()
            report(core, r).wait_send()

    half = subs // 2

    @pl.when(r == 0)
    def _():
        out_ref[0] = back[0, :half, :]
        out_ref[1] = back[1, :half, :]

    @pl.when(r == 1)
    def _():
        out_ref[0] = back[0, half:, :]
        out_ref[1] = back[1, half:, :]

    @pl.when(passing)
    def _():
        onward.wait_send()
        aside.wait_send()

    def finish(slab, _):
        @pl.when(slab != me)
        def _():
            for copy in copies(slab, here):
                copy.wait_send()

        return 0

    lax.fori_loop(0, slabs, finish, 0)


def body(initial, dynamics, obs_rows, obs_values, obs_slab):
    time_devs = lax.axis_size("tm")
    row_devs = lax.axis_size("row")
    width = dynamics.shape[1]
    count, local = obs_rows.shape
    slabs = time_devs * row_devs
    subs = width // LANES
    tiles = width // 256
    vmem = pl.BlockSpec(memory_space=pltpu.VMEM)
    small = pltpu.VMEM((subs, LANES), jnp.float32)
    square = pltpu.VMEM((width, width), jnp.bfloat16)
    square32 = pltpu.VMEM((width, width), jnp.float32)
    sems = pltpu.SemaphoreType.DMA((slabs,))
    states = pl.pallas_call(
        observer_kernel,
        out_shape=jax.ShapeDtypeStruct((2, subs // 2, LANES), jnp.float32),
        in_specs=[vmem, vmem, vmem, pl.BlockSpec(memory_space=pl.ANY), vmem],
        out_specs=vmem,
        scratch_shapes=[
            pltpu.VMEM((slabs, CAP, local), jnp.bfloat16),
            pltpu.VMEM((slabs, 1, LANES), jnp.float32),
            pltpu.VMEM((1, count), jnp.int32),
            pltpu.VMEM((time_devs * CAP, width), jnp.bfloat16),
            pltpu.VMEM((slabs, 1, LANES), jnp.float32),
            square32,
            square,
            square,
            pltpu.VMEM((width, 256), jnp.bfloat16),
            square32,
            pltpu.VMEM((8, width), jnp.float32),
            square,
            square,
            small,
            pltpu.VMEM((LANES, subs, width), jnp.float32),
            square,
            square,
            small,
            small,
            small,
            pltpu.VMEM((2, subs, LANES), jnp.float32),
            small,
            sems,
            sems,
            sems,
            sems,
            pltpu.SemaphoreType.DMA((3,)),
            pltpu.SemaphoreType.DMA((4,)),
            pltpu.SemaphoreType.DMA((3,)),
            pltpu.SemaphoreType.DMA((2, tiles)),
            pltpu.SemaphoreType.DMA((2, tiles)),
            pltpu.SemaphoreType.DMA((2,)),
            pltpu.SemaphoreType.DMA((2,)),
        ],
        compiler_params=pltpu.CompilerParams(
            collective_id=0, has_side_effects=True, vmem_limit_bytes=60 << 20
        ),
        name="observer",
    )(
        obs_slab.reshape(1, -1),
        obs_rows,
        obs_values.reshape(1, -1),
        dynamics,
        initial.reshape(subs, LANES),
    )
    return states.reshape(2, width // 2)


def solution(mesh):
    placed = (P(), P(), P("tm", "row"), P("tm"), P("tm", None))
    return jax.shard_map(
        body, mesh=mesh, in_specs=placed, out_specs=P("tm", "row"), check_vma=False
    )
```

```python
import jax
import jax.numpy as jnp
from jax import lax
from jax.experimental import pallas as pl
from jax.experimental.pallas import tpu as pltpu
from jax.sharding import PartitionSpec as P

CAP = 64
LANES = 128
MESH = pl.DeviceIdType.MESH

sigma_gain = 0.3


def visit(own, turn, total):
    if total & (total - 1):
        return lax.rem(own + turn, total)
    return own ^ turn


def chip_at(place, planes):
    column = place // planes
    depth = lax.rem(place, planes)
    depth = jnp.where(column & 1 == 1, depth, planes - 1 - depth)
    turn = (column + 3) & 3
    return depth * 4 + (turn ^ (turn >> 1))


def place_of(chip, planes):
    depth, turn = chip // 4, chip & 3
    column = ((turn ^ (turn >> 1)) + 1) & 3
    depth = jnp.where(column & 1 == 1, depth, planes - 1 - depth)
    return column * planes + depth


def observer_kernel(
    target_ref, rows_hbm, values_ref, dynamics_ref, start_ref, out_ref,
    rows_ref, values_row, sent, sent_values, slot_ref, got, got_values, dynamics, dyn_high, turned, gain, moment,
    whole, left, lent_left, right, lent_right, b_ref, b_got, came, went, middle, back,
    row_send, row_recv, value_send, value_recv, own_sem, lend_sem, tile_send, tile_recv, pass_send, pass_recv,
    out_send, out_recv,
):
    time_devs, row_devs = lax.axis_size("tm"), lax.axis_size("row")
    t, r = lax.axis_index("tm"), lax.axis_index("row")
    slabs = time_devs * row_devs
    last = time_devs - 1
    planes = time_devs // 4
    place_here = place_of(t, planes)
    after = chip_at(jnp.minimum(place_here + 1, last), planes)
    me = place_here * row_devs + r
    here = t * row_devs + r
    partner = (t, 1 - r)
    count, local = rows_ref.shape
    width = local * row_devs
    subs = width // LANES
    tile = 256
    tiles = width // tile
    block = 256
    share = block // CAP
    blocks = slabs // share

    def device(slab):
        return (chip_at(slab // row_devs, planes), lax.rem(slab, row_devs))

    barrier = pltpu.get_barrier_semaphore()

    def greet(slab, _):
        @pl.when(slab != me)
        def _():
            pl.semaphore_signal(barrier, inc=1, device_id=device(slab), device_id_type=MESH)

        return 0

    lax.fori_loop(0, slabs, greet, 0)
    rows_in = pltpu.make_async_copy(rows_hbm, rows_ref, own_sem.at[3])
    rows_in.start()
    fetch = pltpu.make_async_copy(dynamics_ref, dynamics, own_sem.at[2])
    fetch.start()

    before = (
        lax.broadcasted_iota(jnp.int32, (block, block), 0)
        < lax.broadcasted_iota(jnp.int32, (block, block), 1)
    ).astype(jnp.float32).astype(jnp.bfloat16)
    slab_of = lax.broadcasted_iota(jnp.int32, (slabs, block), 0)
    carry = (slab_of[:, :1] * CAP).astype(jnp.float32)
    for start in range(0, count, block):
        named = (target_ref[:, start : start + block] == slab_of).astype(jnp.float32)
        ahead = jnp.dot(named.astype(jnp.bfloat16), before, preferred_element_type=jnp.float32)
        slot = jnp.sum(named * (ahead + carry), axis=0, keepdims=True)
        slot_ref[:, start : start + block] = slot.astype(jnp.int32)
        carry = carry + jnp.sum(named, axis=1, keepdims=True)

    spread = values_ref[...].astype(jnp.float32)
    for line in range(count // LANES):
        values_row[:, line * LANES : (line + 1) * LANES] = spread[line : line + 1, :]
    values = jnp.broadcast_to(values_row[...], (8, count)).astype(jnp.bfloat16)
    sent_values[...] = jnp.zeros_like(sent_values)

    def landing(source):
        rows = pl.ds(pl.multiple_of(source // row_devs * CAP, CAP), CAP)
        cols = pl.ds(pl.multiple_of(lax.rem(source, row_devs) * local, local), local)
        return got.at[rows, cols]

    def copies(slab, source):
        rows = pltpu.make_async_remote_copy(
            src_ref=sent.at[slab], dst_ref=landing(source),
            send_sem=row_send.at[slab], recv_sem=row_recv.at[source],
            device_id=device(slab), device_id_type=MESH,
        )
        tags = pltpu.make_async_remote_copy(
            src_ref=sent_values.at[slab], dst_ref=got_values.at[source],
            send_sem=value_send.at[slab], recv_sem=value_recv.at[source],
            device_id=device(slab), device_id_type=MESH,
        )
        return rows, tags

    keep = (
        pltpu.make_async_copy(sent.at[me], landing(here), own_sem.at[0]),
        pltpu.make_async_copy(sent_values.at[me], got_values.at[here], own_sem.at[1]),
    )

    def place(at):
        first = at * share
        wanted = lax.broadcasted_iota(jnp.int32, (block, count), 0) + first * CAP
        pick = (wanted == slot_ref[...]).astype(jnp.float32).astype(jnp.bfloat16)
        rows = jnp.dot(pick, rows_ref[...], preferred_element_type=jnp.float32).astype(jnp.bfloat16)
        tags = lax.dot_general(
            values, pick, (((1,), (1,)), ((), ())), preferred_element_type=jnp.float32
        )[:1]
        for inner in range(share):
            sent[first + inner] = rows[inner * CAP : (inner + 1) * CAP]
            sent_values[first + inner, :, :CAP] = tags[:, inner * CAP : (inner + 1) * CAP]

    column_blocks = planes * row_devs // share
    depth = t // 4

    def order(turn):
        column = turn // column_blocks
        along = jnp.where(column & 1 == 1, depth, planes - 1 - depth)
        own = along * row_devs // share
        return column * column_blocks + (own ^ lax.rem(turn, column_blocks)), along

    def send(turn):
        at, along = order(turn)
        key = lax.rem(along * row_devs, share) + r
        for inner in range(share):
            slab = at * share + (key ^ inner)

            @pl.when(slab != me)
            def _():
                rows, tags = copies(slab, here)
                rows.start()

                @pl.when(r == 0)
                def _():
                    tags.start()

            @pl.when(slab == me)
            def _():
                for copy in keep:
                    copy.start()

    rows_in.wait()
    place(order(0)[0])
    pl.semaphore_wait(barrier, slabs - 1)
    send(0)

    def step(turn, _):
        place(order(turn)[0])
        send(turn)
        return 0

    lax.fori_loop(1, blocks, step, 0)

    fetch.wait()

    def divide(k, _):
        rows = pl.ds(pl.multiple_of(k * LANES, LANES), LANES)
        high = dynamics[rows, :].astype(jnp.bfloat16)
        dyn_high[rows, :] = high
        return 0

    lax.fori_loop(0, subs, divide, 0)
    gain[...] = jnp.zeros_like(gain)
    moment[...] = jnp.zeros_like(moment)

    chips = block // CAP
    groups = time_devs // chips
    nearest = t // chips

    def gather(turn, _):
        at = visit(nearest, turn, groups)

        def arrive(source, _):
            @pl.when(source != here)
            def _():
                rows, tags = copies(me, source)
                rows.wait_recv()

                @pl.when(lax.rem(source, row_devs) == 0)
                def _():
                    tags.wait_recv()

            @pl.when(source == here)
            def _():
                for copy in keep:
                    copy.wait()

            return 0

        lax.fori_loop(at * chips * row_devs, (at + 1) * chips * row_devs, arrive, 0)
        own = pl.ds(pl.multiple_of(at * block, block), block)
        rows = got[own, :]
        flipped = rows.T
        turned[:, :block] = flipped
        turned[:, block:] = flipped
        tags = jnp.concatenate(
            [got_values[(at * chips + k) * row_devs][:, :CAP] for k in range(chips)], axis=1
        )
        tags = jnp.broadcast_to(tags, (8, block)).astype(jnp.bfloat16)
        moment[...] += jnp.dot(tags, rows, preferred_element_type=jnp.float32)

        def column(k, _):
            cols = pl.ds(pl.multiple_of(k * tile, tile), tile)
            moved = jnp.dot(got[own, :], dyn_high[:, cols], preferred_element_type=jnp.float32)
            both = jnp.concatenate([got[own, cols], moved.astype(jnp.bfloat16)], axis=0)
            gain[:, cols] += jnp.dot(turned[...], both, preferred_element_type=jnp.float32)
            return 0

        lax.fori_loop(0, tiles, column, 0)
        return 0

    lax.fori_loop(0, groups, gather, 0)

    half = width // 2
    near = tiles // 2

    def push(source, target, send_sem, recv_sem, peer):
        return pltpu.make_async_remote_copy(
            src_ref=source, dst_ref=target, send_sem=send_sem, recv_sem=recv_sem,
            device_id=peer, device_id_type=MESH,
        )

    lend = push(b_ref, b_got, lend_sem.at[0], lend_sem.at[1], partner)

    def columns(k):
        return pl.ds(pl.multiple_of(k * tile, tile), tile)

    def left_part(j):
        return [
            push(
                lent_left.at[j, :, bits], left.at[j, :, bits],
                tile_send.at[i, j], tile_recv.at[i, j], partner,
            )
            for i, bits in enumerate((slice(0, tile), slice(tile, 2 * tile)))
        ]

    def right_part(k):
        return [
            push(
                lent_right.at[i, :, columns(k)], right.at[i, :, columns(k)],
                tile_send.at[i, k], tile_recv.at[i, k], partner,
            )
            for i in range(2)
        ]

    for sub in range(subs):
        b_ref[sub : sub + 1, :] = sigma_gain * moment[:1, sub * LANES : (sub + 1) * LANES]

    def settled(own, cols):
        change = dynamics[own, cols] - sigma_gain * gain[own, cols]
        gain[own, cols] = change
        high = change.astype(jnp.bfloat16)
        return high, (change - high.astype(jnp.float32)).astype(jnp.bfloat16)

    @pl.when(r == 0)
    def _():
        lend.start()

        def settle(k, _):
            cols = columns(k)
            high, low = settled(slice(half, width), cols)
            lent_right[0, :, cols] = high
            lent_right[1, :, cols] = low
            for copy in right_part(k):
                copy.start()
            high, low = settled(slice(0, half), cols)
            right[0, :, cols] = high
            right[1, :, cols] = low
            return 0

        lax.fori_loop(0, tiles, settle, 0)

    @pl.when(r == 1)
    def _():
        def settle_far(j, _):
            for own in (slice(0, half), slice(half, width)):
                high, low = settled(own, columns(j))
                lent_left[j, own, :tile] = high
                lent_left[j, own, tile:] = low
            for copy in left_part(j):
                copy.start()
            return 0

        lax.fori_loop(0, near, settle_far, 0)

        def settle_near(j, _):
            for own in (slice(0, half), slice(half, width)):
                high, low = settled(own, columns(j + near))
                left[j, own, :tile] = high
                left[j, own, tile:] = low
            return 0

        lax.fori_loop(0, near, settle_near, 0)

    lane = lax.broadcasted_iota(jnp.int32, (subs, LANES), 1)
    line = lax.broadcasted_iota(jnp.int32, (subs, LANES), 0)
    group = 16

    def apply(matrix, vector):
        pieces = [jnp.broadcast_to(vector[k : k + 1, :], (subs, LANES)) for k in range(subs)]

        def rows(step, total):
            for inner in range(group):
                g = step * group + inner
                own = pl.ds(pl.multiple_of(g * subs, subs), subs)
                part = matrix[own, 0:LANES] * pieces[0]
                for k in range(1, subs):
                    part = part + matrix[own, k * LANES : (k + 1) * LANES] * pieces[k]
                total = jnp.where(lane == g, jnp.sum(part, axis=1, keepdims=True), total)
            return total

        total = lax.fori_loop(0, LANES // group, rows, jnp.zeros((subs, LANES), jnp.float32))
        result = jnp.zeros((subs, LANES), jnp.float32)
        for k in range(subs):
            spots = lane // subs + k * (LANES // subs)
            moved = jnp.take_along_axis(total, spots, axis=1)
            kept = jnp.where(line == lax.rem(lane, subs), moved, 0.0)
            result = jnp.where(line == k, jnp.sum(kept, axis=0, keepdims=True), result)
        return result

    def product(j, cols):
        own = pl.ds(pl.multiple_of(j * tile, tile), tile)
        high, low = right[0, own, cols], right[1, own, cols]
        return jnp.dot(
            left[j], jnp.concatenate([high, high], axis=0), preferred_element_type=jnp.float32
        ) + jnp.dot(left[j, :, :tile], low, preferred_element_type=jnp.float32)

    @pl.when(r == 0)
    def _():
        def compose(j, _):
            for copy in left_part(j):
                copy.wait_recv()

            def fill(k, _):
                cols = columns(k)

                @pl.when(j == 0)
                def _():
                    whole[:, cols] = gain[:, cols] + product(j, cols)

                @pl.when(j > 0)
                def _():
                    whole[:, cols] += product(j, cols)

                return 0

            lax.fori_loop(0, tiles, fill, 0)
            return 0

        lax.fori_loop(0, near, compose, 0)
        lend.wait_send()

        def drain(k, _):
            for copy in right_part(k):
                copy.wait_send()
            return 0

        lax.fori_loop(0, tiles, drain, 0)

    @pl.when(r == 1)
    def _():
        lend.wait_recv()
        b_ref[...] += apply(gain, b_got[...])

        def compose(k, _):
            for copy in right_part(k):
                copy.wait_recv()
            cols = columns(k)
            total = gain[:, cols] + product(0, cols)
            for j in range(1, near):
                total = total + product(j, cols)
            whole[:, cols] = total
            return 0

        lax.fori_loop(0, tiles, compose, 0)

        def drain(j, _):
            for copy in left_part(j):
                copy.wait_send()
            return 0

        lax.fori_loop(0, near, drain, 0)

    def onward(core, sender):
        return push(
            went, came.at[sender], pass_send.at[core], pass_recv.at[sender], (after, core)
        )

    @pl.when(place_here == 0)
    def _():
        came[0] = start_ref[...]
        came[1] = jnp.zeros_like(start_ref)

    @pl.when(place_here > 0)
    def _():
        for core in range(2):
            onward(core, core).wait_recv()

    state = came[0] + came[1]
    share_of = jnp.where(r == 0, 1.0, 0.0)
    went[...] = apply(whole, state) + (b_ref[...] + share_of * state)
    passing = place_here < last

    @pl.when(passing)
    def _():
        for core in range(2):
            onward(core, r).start()

    stays = place_here == t

    def report(source, core, slot):
        return push(
            source, back.at[slot], out_send.at[slot, core], out_recv.at[slot], (place_here, core)
        )

    def tell(source, slot):
        for core in range(2):
            @pl.when(jnp.logical_not(stays & (r == core)))
            def _():
                report(source, core, slot).start()

            @pl.when(stays & (r == core))
            def _():
                back[slot] = source[...]

    @pl.when(r == 0)
    def _():
        tell(went, 1)
        middle[...] = apply(gain, state) + (b_ref[...] + state)
        tell(middle, 0)

    @pl.when(r == 1)
    def _():
        tell(went, 2)

    for slot, sender in ((1, 0), (2, 1), (0, 0)):
        @pl.when(jnp.logical_not(stays & (r == sender)))
        def _():
            report(went, r, slot).wait_recv()

    for core in range(2):
        @pl.when(jnp.logical_not(stays & (r == core)))
        def _():
            @pl.when(r == 0)
            def _():
                report(went, core, 1).wait_send()
                report(middle, core, 0).wait_send()

            @pl.when(r == 1)
            def _():
                report(went, core, 2).wait_send()

    part = subs // 2

    @pl.when(r == 0)
    def _():
        out_ref[0] = back[0, :part, :]
        out_ref[1] = back[1, :part, :] + back[2, :part, :]

    @pl.when(r == 1)
    def _():
        out_ref[0] = back[0, part:, :]
        out_ref[1] = back[1, part:, :] + back[2, part:, :]

    @pl.when(passing)
    def _():
        for core in range(2):
            onward(core, r).wait_send()

    def finish(slab, _):
        @pl.when(slab != me)
        def _():
            rows, tags = copies(slab, here)
            rows.wait_send()

            @pl.when(r == 0)
            def _():
                tags.wait_send()

        return 0

    lax.fori_loop(0, slabs, finish, 0)


def body(initial, dynamics, obs_rows, obs_values, obs_slab):
    time_devs = lax.axis_size("tm")
    row_devs = lax.axis_size("row")
    width = dynamics.shape[1]
    count, local = obs_rows.shape
    slabs = time_devs * row_devs
    subs = width // LANES
    tiles = width // 256
    vmem = pl.BlockSpec(memory_space=pltpu.VMEM)
    anywhere = pl.BlockSpec(memory_space=pl.ANY)
    small = pltpu.VMEM((subs, LANES), jnp.float32)
    square = pltpu.VMEM((width, width), jnp.float32)
    columns = pltpu.VMEM((tiles // 2, width, 512), jnp.bfloat16)
    lines = pltpu.VMEM((2, width // 2, width), jnp.bfloat16)
    sems = pltpu.SemaphoreType.DMA((slabs,))
    states = pl.pallas_call(
        observer_kernel,
        out_shape=jax.ShapeDtypeStruct((2, subs // 2, LANES), jnp.float32),
        in_specs=[vmem, anywhere, vmem, anywhere, vmem],
        out_specs=vmem,
        scratch_shapes=[
            pltpu.VMEM((count, local), jnp.bfloat16),
            pltpu.VMEM((1, count), jnp.float32),
            pltpu.VMEM((slabs, CAP, local), jnp.bfloat16),
            pltpu.VMEM((slabs, 1, LANES), jnp.float32),
            pltpu.VMEM((1, count), jnp.int32),
            pltpu.VMEM((time_devs * CAP, width), jnp.bfloat16),
            pltpu.VMEM((slabs, 1, LANES), jnp.float32),
            square,
            pltpu.VMEM((width, width), jnp.bfloat16),
            pltpu.VMEM((width, 512), jnp.bfloat16),
            square,
            pltpu.VMEM((8, width), jnp.float32),
            square,
            columns,
            columns,
            lines,
            lines,
            small,
            small,
            pltpu.VMEM((2, subs, LANES), jnp.float32),
            small,
            small,
            pltpu.VMEM((3, subs, LANES), jnp.float32),
            sems,
            sems,
            sems,
            sems,
            pltpu.SemaphoreType.DMA((4,)),
            pltpu.SemaphoreType.DMA((2,)),
            pltpu.SemaphoreType.DMA((2, tiles)),
            pltpu.SemaphoreType.DMA((2, tiles)),
            pltpu.SemaphoreType.DMA((2,)),
            pltpu.SemaphoreType.DMA((2,)),
            pltpu.SemaphoreType.DMA((3, 2)),
            pltpu.SemaphoreType.DMA((3,)),
        ],
        compiler_params=pltpu.CompilerParams(
            collective_id=0, has_side_effects=True, vmem_limit_bytes=60 << 20
        ),
        name="observer",
    )(
        obs_slab.reshape(1, -1),
        obs_rows,
        obs_values.reshape(-1, LANES),
        dynamics,
        initial.reshape(subs, LANES),
    )
    return states.reshape(2, width // 2)


def solution(mesh):
    placed = (P(), P(), P("tm", "row"), P("tm"), P("tm", None))
    return jax.shard_map(
        body, mesh=mesh, in_specs=placed, out_specs=P("tm", "row"), check_vma=False
    )
```

```python
import jax
import jax.numpy as jnp
from jax import lax
from jax.experimental import pallas as pl
from jax.experimental.pallas import tpu as pltpu
from jax.sharding import PartitionSpec as P

CAP = 64
LANES = 128
MESH = pl.DeviceIdType.MESH

sigma_gain = 0.3


def visit(own, turn, total):
    if total & (total - 1):
        return lax.rem(own + turn, total)
    return own ^ turn


def chip_at(place, planes):
    column = place // planes
    depth = lax.rem(place, planes)
    depth = jnp.where(column & 1 == 1, depth, planes - 1 - depth)
    turn = (column + 3) & 3
    return depth * 4 + (turn ^ (turn >> 1))


def place_of(chip, planes):
    depth, turn = chip // 4, chip & 3
    column = ((turn ^ (turn >> 1)) + 1) & 3
    depth = jnp.where(column & 1 == 1, depth, planes - 1 - depth)
    return column * planes + depth


def observer_kernel(
    target_ref, rows_hbm, values_ref, dynamics_ref, start_ref, out_ref,
    rows_ref, values_row, sent, sent_values, slot_ref, got, got_values, dynamics, dyn_high, turned, gain, moment,
    whole, halves, right, b_ref, b_got, came, went, back,
    row_send, row_recv, value_send, value_recv, own_sem, lend_sem, tile_send, tile_recv, pass_send, pass_recv,
    out_send, out_recv,
):
    time_devs, row_devs = lax.axis_size("tm"), lax.axis_size("row")
    t, r = lax.axis_index("tm"), lax.axis_index("row")
    slabs = time_devs * row_devs
    last = time_devs - 1
    planes = time_devs // 4
    place_here = place_of(t, planes)
    after = chip_at(jnp.minimum(place_here + 1, last), planes)
    me = place_here * row_devs + r
    here = t * row_devs + r
    partner = (t, 1 - r)
    count, local = rows_ref.shape
    width = local * row_devs
    subs = width // LANES
    tile = 256
    tiles = width // tile
    block = 256
    share = block // CAP
    blocks = slabs // share

    def device(slab):
        return (chip_at(slab // row_devs, planes), lax.rem(slab, row_devs))

    barrier = pltpu.get_barrier_semaphore()

    def greet(slab, _):
        @pl.when(slab != me)
        def _():
            pl.semaphore_signal(barrier, inc=1, device_id=device(slab), device_id_type=MESH)

        return 0

    lax.fori_loop(0, slabs, greet, 0)
    rows_in = pltpu.make_async_copy(rows_hbm, rows_ref, own_sem.at[3])
    rows_in.start()
    fetch = pltpu.make_async_copy(dynamics_ref, dynamics, own_sem.at[2])
    fetch.start()

    before = (
        lax.broadcasted_iota(jnp.int32, (block, block), 0)
        < lax.broadcasted_iota(jnp.int32, (block, block), 1)
    ).astype(jnp.float32).astype(jnp.bfloat16)
    slab_of = lax.broadcasted_iota(jnp.int32, (slabs, block), 0)
    carry = (slab_of[:, :1] * CAP).astype(jnp.float32)
    for start in range(0, count, block):
        named = (target_ref[:, start : start + block] == slab_of).astype(jnp.float32)
        ahead = jnp.dot(named.astype(jnp.bfloat16), before, preferred_element_type=jnp.float32)
        slot = jnp.sum(named * (ahead + carry), axis=0, keepdims=True)
        slot_ref[:, start : start + block] = slot.astype(jnp.int32)
        carry = carry + jnp.sum(named, axis=1, keepdims=True)

    spread = values_ref[...].astype(jnp.float32)
    for line in range(count // LANES):
        values_row[:, line * LANES : (line + 1) * LANES] = spread[line : line + 1, :]
    values = jnp.broadcast_to(values_row[...], (8, count)).astype(jnp.bfloat16)
    sent_values[...] = jnp.zeros_like(sent_values)

    def landing(source):
        rows = pl.ds(pl.multiple_of(source // row_devs * CAP, CAP), CAP)
        cols = pl.ds(pl.multiple_of(lax.rem(source, row_devs) * local, local), local)
        return got.at[rows, cols]

    def copies(slab, source):
        rows = pltpu.make_async_remote_copy(
            src_ref=sent.at[slab], dst_ref=landing(source),
            send_sem=row_send.at[slab], recv_sem=row_recv.at[source],
            device_id=device(slab), device_id_type=MESH,
        )
        tags = pltpu.make_async_remote_copy(
            src_ref=sent_values.at[slab], dst_ref=got_values.at[source],
            send_sem=value_send.at[slab], recv_sem=value_recv.at[source],
            device_id=device(slab), device_id_type=MESH,
        )
        return rows, tags

    keep = (
        pltpu.make_async_copy(sent.at[me], landing(here), own_sem.at[0]),
        pltpu.make_async_copy(sent_values.at[me], got_values.at[here], own_sem.at[1]),
    )

    def place(at):
        first = at * share
        wanted = lax.broadcasted_iota(jnp.int32, (block, count), 0) + first * CAP
        pick = (wanted == slot_ref[...]).astype(jnp.float32).astype(jnp.bfloat16)
        rows = jnp.dot(pick, rows_ref[...], preferred_element_type=jnp.float32).astype(jnp.bfloat16)
        tags = lax.dot_general(
            values, pick, (((1,), (1,)), ((), ())), preferred_element_type=jnp.float32
        )[:1]
        for inner in range(share):
            sent[first + inner] = rows[inner * CAP : (inner + 1) * CAP]
            sent_values[first + inner, :, :CAP] = tags[:, inner * CAP : (inner + 1) * CAP]

    column_blocks = planes * row_devs // share
    depth = t // 4

    def order(turn):
        column = turn // column_blocks
        along = jnp.where(column & 1 == 1, depth, planes - 1 - depth)
        own = along * row_devs // share
        return column * column_blocks + (own ^ lax.rem(turn, column_blocks)), along

    def send(turn):
        at, along = order(turn)
        key = lax.rem(along * row_devs, share) + r
        for inner in range(share):
            slab = at * share + (key ^ inner)

            @pl.when(slab != me)
            def _():
                rows, tags = copies(slab, here)
                rows.start()

                @pl.when(r == 0)
                def _():
                    tags.start()

            @pl.when(slab == me)
            def _():
                for copy in keep:
                    copy.start()

    rows_in.wait()
    place(order(0)[0])
    pl.semaphore_wait(barrier, slabs - 1)
    send(0)

    def step(turn, _):
        place(order(turn)[0])
        send(turn)
        return 0

    lax.fori_loop(1, blocks, step, 0)

    fetch.wait()

    def divide(k, _):
        rows = pl.ds(pl.multiple_of(k * LANES, LANES), LANES)
        high = dynamics[rows, :].astype(jnp.bfloat16)
        dyn_high[rows, :] = high
        return 0

    lax.fori_loop(0, subs, divide, 0)
    gain[...] = jnp.zeros_like(gain)
    moment[...] = jnp.zeros_like(moment)

    chips = block // CAP
    groups = time_devs // chips
    nearest = t // chips

    def gather(turn, _):
        at = visit(nearest, turn, groups)

        def arrive(source, _):
            @pl.when(source != here)
            def _():
                rows, tags = copies(me, source)
                rows.wait_recv()

                @pl.when(lax.rem(source, row_devs) == 0)
                def _():
                    tags.wait_recv()

            @pl.when(source == here)
            def _():
                for copy in keep:
                    copy.wait()

            return 0

        lax.fori_loop(at * chips * row_devs, (at + 1) * chips * row_devs, arrive, 0)
        own = pl.ds(pl.multiple_of(at * block, block), block)
        rows = got[own, :]
        flipped = rows.T
        turned[:, :block] = flipped
        turned[:, block:] = flipped
        tags = jnp.concatenate(
            [got_values[(at * chips + k) * row_devs][:, :CAP] for k in range(chips)], axis=1
        )
        tags = jnp.broadcast_to(tags, (8, block)).astype(jnp.bfloat16)
        moment[...] += jnp.dot(tags, rows, preferred_element_type=jnp.float32)

        def column(k, _):
            cols = pl.ds(pl.multiple_of(k * tile, tile), tile)
            moved = jnp.dot(got[own, :], dyn_high[:, cols], preferred_element_type=jnp.float32)
            both = jnp.concatenate([got[own, cols], moved.astype(jnp.bfloat16)], axis=0)
            gain[:, cols] += jnp.dot(turned[...], both, preferred_element_type=jnp.float32)
            return 0

        lax.fori_loop(0, tiles, column, 0)
        return 0

    lax.fori_loop(0, groups, gather, 0)

    def push(source, target, send_sem, recv_sem, peer):
        return pltpu.make_async_remote_copy(
            src_ref=source, dst_ref=target, send_sem=send_sem, recv_sem=recv_sem,
            device_id=peer, device_id_type=MESH,
        )

    lend = push(b_ref, b_got, lend_sem.at[0], lend_sem.at[1], partner)

    def columns(k):
        return pl.ds(pl.multiple_of(k * tile, tile), tile)

    def part(k):
        return [
            push(
                halves.at[i, :, columns(k)], right.at[i, :, columns(k)],
                tile_send.at[i, k], tile_recv.at[i, k], partner,
            )
            for i in range(2)
        ]

    for sub in range(subs):
        b_ref[sub : sub + 1, :] = sigma_gain * moment[:1, sub * LANES : (sub + 1) * LANES]

    @pl.when(r == 0)
    def _():
        lend.start()

    def settle(k, _):
        cols = columns(k)
        change = dynamics[:, cols] - sigma_gain * gain[:, cols]
        gain[:, cols] = change
        high = change.astype(jnp.bfloat16)
        halves[0, :, cols] = high
        halves[1, :, cols] = (change - high.astype(jnp.float32)).astype(jnp.bfloat16)

        @pl.when(r == 0)
        def _():
            for copy in part(k):
                copy.start()

        return 0

    lax.fori_loop(0, tiles, settle, 0)

    lane = lax.broadcasted_iota(jnp.int32, (subs, LANES), 1)
    line = lax.broadcasted_iota(jnp.int32, (subs, LANES), 0)
    group = 64

    def apply(matrix, vector):
        pieces = [jnp.broadcast_to(vector[k : k + 1, :], (subs, LANES)) for k in range(subs)]

        def rows(step, total):
            for inner in range(group):
                g = step * group + inner
                own = pl.ds(pl.multiple_of(g * subs, subs), subs)
                part = matrix[own, 0:LANES] * pieces[0]
                for k in range(1, subs):
                    part = part + matrix[own, k * LANES : (k + 1) * LANES] * pieces[k]
                total = jnp.where(lane == g, jnp.sum(part, axis=1, keepdims=True), total)
            return total

        total = lax.fori_loop(0, LANES // group, rows, jnp.zeros((subs, LANES), jnp.float32))
        result = jnp.zeros((subs, LANES), jnp.float32)
        for k in range(subs):
            spots = lane // subs + k * (LANES // subs)
            moved = jnp.take_along_axis(total, spots, axis=1)
            kept = jnp.where(line == lax.rem(lane, subs), moved, 0.0)
            result = jnp.where(line == k, jnp.sum(kept, axis=0, keepdims=True), result)
        return result

    @pl.when(r == 0)
    def _():
        lend.wait_send()

        def drain(k, _):
            for copy in part(k):
                copy.wait_send()
            return 0

        lax.fori_loop(0, tiles, drain, 0)

    @pl.when(r == 1)
    def _():
        lend.wait_recv()
        b_ref[...] += b_got[...] + apply(gain, b_got[...])

        def compose(k, _):
            for copy in part(k):
                copy.wait_recv()
            cols = columns(k)
            high, low = right[0, :, cols], right[1, :, cols]
            whole[:, cols] = (
                gain[:, cols] + (high.astype(jnp.float32) + low.astype(jnp.float32))
                + jnp.dot(halves[0], high, preferred_element_type=jnp.float32)
                + jnp.dot(halves[0], low, preferred_element_type=jnp.float32)
                + jnp.dot(halves[1], high, preferred_element_type=jnp.float32)
            )
            return 0

        lax.fori_loop(0, tiles, compose, 0)

    onward = push(went, came, pass_send.at[1], pass_recv.at[0], (after, 1))
    aside = push(went, came, pass_send.at[0], pass_recv.at[0], (after, 0))

    @pl.when(place_here == 0)
    def _():
        came[...] = start_ref[...]

    @pl.when(place_here > 0)
    def _():
        onward.wait_recv()

    passing = (r == 1) & (place_here < last)

    @pl.when(r == 1)
    def _():
        state = came[...]
        went[...] = apply(whole, state) + (b_ref[...] + state)

    @pl.when(passing)
    def _():
        onward.start()
        aside.start()

    @pl.when(r == 0)
    def _():
        state = came[...]
        went[...] = apply(gain, state) + (b_ref[...] + state)

    stays = place_here == t

    def report(core, sender):
        return push(
            went, back.at[sender], out_send.at[core], out_recv.at[sender], (place_here, core)
        )

    for core in range(2):
        @pl.when(jnp.logical_not(stays & (r == core)))
        def _():
            report(core, r).start()

        @pl.when(stays & (r == core))
        def _():
            back[core] = went[...]

    for core in range(2):
        @pl.when(jnp.logical_not(stays & (r == core)))
        def _():
            report(core, core).wait_recv()
            report(core, r).wait_send()

    part = subs // 2

    @pl.when(r == 0)
    def _():
        out_ref[0] = back[0, :part, :]
        out_ref[1] = back[1, :part, :]

    @pl.when(r == 1)
    def _():
        out_ref[0] = back[0, part:, :]
        out_ref[1] = back[1, part:, :]

    @pl.when(passing)
    def _():
        onward.wait_send()
        aside.wait_send()

    def finish(slab, _):
        @pl.when(slab != me)
        def _():
            rows, tags = copies(slab, here)
            rows.wait_send()

            @pl.when(r == 0)
            def _():
                tags.wait_send()

        return 0

    lax.fori_loop(0, slabs, finish, 0)


def body(initial, dynamics, obs_rows, obs_values, obs_slab):
    time_devs = lax.axis_size("tm")
    row_devs = lax.axis_size("row")
    width = dynamics.shape[1]
    count, local = obs_rows.shape
    slabs = time_devs * row_devs
    subs = width // LANES
    tiles = width // 256
    vmem = pl.BlockSpec(memory_space=pltpu.VMEM)
    anywhere = pl.BlockSpec(memory_space=pl.ANY)
    small = pltpu.VMEM((subs, LANES), jnp.float32)
    square = pltpu.VMEM((width, width), jnp.float32)
    halves = pltpu.VMEM((2, width, width), jnp.bfloat16)
    sems = pltpu.SemaphoreType.DMA((slabs,))
    states = pl.pallas_call(
        observer_kernel,
        out_shape=jax.ShapeDtypeStruct((2, subs // 2, LANES), jnp.float32),
        in_specs=[vmem, anywhere, vmem, anywhere, vmem],
        out_specs=vmem,
        scratch_shapes=[
            pltpu.VMEM((count, local), jnp.bfloat16),
            pltpu.VMEM((1, count), jnp.float32),
            pltpu.VMEM((slabs, CAP, local), jnp.bfloat16),
            pltpu.VMEM((slabs, 1, LANES), jnp.float32),
            pltpu.VMEM((1, count), jnp.int32),
            pltpu.VMEM((time_devs * CAP, width), jnp.bfloat16),
            pltpu.VMEM((slabs, 1, LANES), jnp.float32),
            square,
            pltpu.VMEM((width, width), jnp.bfloat16),
            pltpu.VMEM((width, 512), jnp.bfloat16),
            square,
            pltpu.VMEM((8, width), jnp.float32),
            square,
            halves,
            halves,
            small,
            small,
            small,
            small,
            pltpu.VMEM((2, subs, LANES), jnp.float32),
            sems,
            sems,
            sems,
            sems,
            pltpu.SemaphoreType.DMA((4,)),
            pltpu.SemaphoreType.DMA((2,)),
            pltpu.SemaphoreType.DMA((2, tiles)),
            pltpu.SemaphoreType.DMA((2, tiles)),
            pltpu.SemaphoreType.DMA((2,)),
            pltpu.SemaphoreType.DMA((1,)),
            pltpu.SemaphoreType.DMA((2,)),
            pltpu.SemaphoreType.DMA((2,)),
        ],
        compiler_params=pltpu.CompilerParams(
            collective_id=0, has_side_effects=True, vmem_limit_bytes=60 << 20
        ),
        name="observer",
    )(
        obs_slab.reshape(1, -1),
        obs_rows,
        obs_values.reshape(-1, LANES),
        dynamics,
        initial.reshape(subs, LANES),
    )
    return states.reshape(2, width // 2)


def solution(mesh):
    placed = (P(), P(), P("tm", "row"), P("tm"), P("tm", None))
    return jax.shard_map(
        body, mesh=mesh, in_specs=placed, out_specs=P("tm", "row"), check_vma=False
    )
```

```python
import jax
import jax.numpy as jnp
from jax import lax
from jax.experimental import pallas as pl
from jax.experimental.pallas import tpu as pltpu
from jax.sharding import PartitionSpec as P

CAP = 64
LANES = 128
MESH = pl.DeviceIdType.MESH

sigma_gain = 0.3


def visit(own, turn, total):
    if total & (total - 1):
        return lax.rem(own + turn, total)
    return own ^ turn


def chip_at(place, planes):
    column = place // planes
    depth = lax.rem(place, planes)
    depth = jnp.where(column & 1 == 1, depth, planes - 1 - depth)
    turn = (column + 3) & 3
    return depth * 4 + (turn ^ (turn >> 1))


def place_of(chip, planes):
    depth, turn = chip // 4, chip & 3
    column = ((turn ^ (turn >> 1)) + 1) & 3
    depth = jnp.where(column & 1 == 1, depth, planes - 1 - depth)
    return column * planes + depth


def observer_kernel(
    target_ref, rows_hbm, values_ref, dynamics_ref, start_ref, out_ref,
    rows_ref, values_row, sent, sent_values, slot_ref, got, got_values, dynamics, dyn_high, turned, rounded, gain, moment,
    whole, halves, right, b_ref, b_got, came, went, back,
    row_send, row_recv, value_send, value_recv, own_sem, lend_sem, tile_send, tile_recv, pass_send, pass_recv,
    out_send, out_recv,
):
    time_devs, row_devs = lax.axis_size("tm"), lax.axis_size("row")
    t, r = lax.axis_index("tm"), lax.axis_index("row")
    slabs = time_devs * row_devs
    last = time_devs - 1
    planes = time_devs // 4
    place_here = place_of(t, planes)
    after = chip_at(jnp.minimum(place_here + 1, last), planes)
    me = place_here * row_devs + r
    here = t * row_devs + r
    partner = (t, 1 - r)
    count, local = rows_ref.shape
    width = local * row_devs
    subs = width // LANES
    tile = 256
    tiles = width // tile
    wide = 2 * tile
    block = 256
    share = block // CAP
    blocks = slabs // share

    def device(slab):
        return (chip_at(slab // row_devs, planes), lax.rem(slab, row_devs))

    barrier = pltpu.get_barrier_semaphore()

    def greet(slab, _):
        @pl.when(slab != me)
        def _():
            pl.semaphore_signal(barrier, inc=1, device_id=device(slab), device_id_type=MESH)

        return 0

    lax.fori_loop(0, slabs, greet, 0)
    rows_in = pltpu.make_async_copy(rows_hbm, rows_ref, own_sem.at[3])
    rows_in.start()
    fetch = pltpu.make_async_copy(dynamics_ref, dynamics, own_sem.at[2])
    fetch.start()

    before = (
        lax.broadcasted_iota(jnp.int32, (block, block), 0)
        < lax.broadcasted_iota(jnp.int32, (block, block), 1)
    ).astype(jnp.float32).astype(jnp.bfloat16)
    slab_of = lax.broadcasted_iota(jnp.int32, (slabs, block), 0)
    carry = (slab_of[:, :1] * CAP).astype(jnp.float32)
    for start in range(0, count, block):
        named = (target_ref[:, start : start + block] == slab_of).astype(jnp.float32)
        ahead = jnp.dot(named.astype(jnp.bfloat16), before, preferred_element_type=jnp.float32)
        slot = jnp.sum(named * (ahead + carry), axis=0, keepdims=True)
        slot_ref[:, start : start + block] = slot.astype(jnp.int32)
        carry = carry + jnp.sum(named, axis=1, keepdims=True)

    spread = values_ref[...].astype(jnp.float32)
    for line in range(count // LANES):
        values_row[:, line * LANES : (line + 1) * LANES] = spread[line : line + 1, :]
    values = jnp.broadcast_to(values_row[...], (8, count)).astype(jnp.bfloat16)
    sent_values[...] = jnp.zeros_like(sent_values)

    def landing(source):
        rows = pl.ds(pl.multiple_of(source // row_devs * CAP, CAP), CAP)
        cols = pl.ds(pl.multiple_of(lax.rem(source, row_devs) * local, local), local)
        return got.at[rows, cols]

    def copies(slab, source):
        rows = pltpu.make_async_remote_copy(
            src_ref=sent.at[slab], dst_ref=landing(source),
            send_sem=row_send.at[slab], recv_sem=row_recv.at[source],
            device_id=device(slab), device_id_type=MESH,
        )
        tags = pltpu.make_async_remote_copy(
            src_ref=sent_values.at[slab], dst_ref=got_values.at[source],
            send_sem=value_send.at[slab], recv_sem=value_recv.at[source],
            device_id=device(slab), device_id_type=MESH,
        )
        return rows, tags

    keep = (
        pltpu.make_async_copy(sent.at[me], landing(here), own_sem.at[0]),
        pltpu.make_async_copy(sent_values.at[me], got_values.at[here], own_sem.at[1]),
    )

    def place(at):
        first = at * share
        wanted = lax.broadcasted_iota(jnp.int32, (block, count), 0) + first * CAP
        pick = (wanted == slot_ref[...]).astype(jnp.float32).astype(jnp.bfloat16)
        rows = jnp.dot(pick, rows_ref[...], preferred_element_type=jnp.float32).astype(jnp.bfloat16)
        tags = lax.dot_general(
            values, pick, (((1,), (1,)), ((), ())), preferred_element_type=jnp.float32
        )[:1]
        for inner in range(share):
            sent[first + inner] = rows[inner * CAP : (inner + 1) * CAP]
            sent_values[first + inner, :, :CAP] = tags[:, inner * CAP : (inner + 1) * CAP]

    column_blocks = planes * row_devs // share
    depth = t // 4

    def order(turn):
        column = turn // column_blocks
        along = jnp.where(column & 1 == 1, depth, planes - 1 - depth)
        own = along * row_devs // share
        return column * column_blocks + (own ^ lax.rem(turn, column_blocks)), along

    def send(turn):
        at, along = order(turn)
        key = lax.rem(along * row_devs, share) + r
        for inner in range(share):
            slab = at * share + (key ^ inner)

            @pl.when(slab != me)
            def _():
                rows, tags = copies(slab, here)
                rows.start()

                @pl.when(r == 0)
                def _():
                    tags.start()

            @pl.when(slab == me)
            def _():
                for copy in keep:
                    copy.start()

    rows_in.wait()
    place(order(0)[0])
    pl.semaphore_wait(barrier, slabs - 1)
    send(0)

    def step(turn, _):
        place(order(turn)[0])
        send(turn)
        return 0

    lax.fori_loop(1, blocks, step, 0)

    fetch.wait()

    def divide(k, _):
        rows = pl.ds(pl.multiple_of(k * LANES, LANES), LANES)
        high = dynamics[rows, :].astype(jnp.bfloat16)
        dyn_high[rows, :] = high
        return 0

    lax.fori_loop(0, subs, divide, 0)
    gain[...] = jnp.zeros_like(gain)
    moment[...] = jnp.zeros_like(moment)

    chips = block // CAP
    groups = time_devs // chips
    nearest = t // chips

    def gather(turn, _):
        at = visit(nearest, turn, groups)

        def arrive(source, _):
            @pl.when(source != here)
            def _():
                rows, tags = copies(me, source)
                rows.wait_recv()

                @pl.when(lax.rem(source, row_devs) == 0)
                def _():
                    tags.wait_recv()

            @pl.when(source == here)
            def _():
                for copy in keep:
                    copy.wait()

            return 0

        lax.fori_loop(at * chips * row_devs, (at + 1) * chips * row_devs, arrive, 0)
        own = pl.ds(pl.multiple_of(at * block, block), block)
        rows = got[own, :]
        turned[...] = rows.T
        tags = jnp.concatenate(
            [got_values[(at * chips + k) * row_devs][:, :CAP] for k in range(chips)], axis=1
        )
        tags = jnp.broadcast_to(tags, (8, block)).astype(jnp.bfloat16)
        moment[...] += jnp.dot(tags, rows, preferred_element_type=jnp.float32)

        def column(k, _):
            cols = pl.ds(pl.multiple_of(k * wide, wide), wide)
            gain[:, cols] += jnp.dot(turned[...], got[own, cols], preferred_element_type=jnp.float32)
            return 0

        lax.fori_loop(0, width // wide, column, 0)
        return 0

    lax.fori_loop(0, groups, gather, 0)

    def push(source, target, send_sem, recv_sem, peer):
        return pltpu.make_async_remote_copy(
            src_ref=source, dst_ref=target, send_sem=send_sem, recv_sem=recv_sem,
            device_id=peer, device_id_type=MESH,
        )

    lend = push(b_ref, b_got, lend_sem.at[0], lend_sem.at[1], partner)

    def columns(k):
        return pl.ds(pl.multiple_of(k * tile, tile), tile)

    def part(i, k):
        cols = columns(k)
        return push(
            halves.at[i, :, cols], right.at[i, :, cols], tile_send.at[i, k], tile_recv.at[i, k], partner,
        )

    for sub in range(subs):
        b_ref[sub : sub + 1, :] = sigma_gain * moment[:1, sub * LANES : (sub + 1) * LANES]

    for k in range(tiles):
        rows = slice(k * tile, (k + 1) * tile)
        rounded[rows, :] = gain[rows, :].astype(jnp.bfloat16)

    def span(k):
        return pl.ds(pl.multiple_of(k * wide, wide), wide)

    def settle(cols):
        moved = jnp.dot(rounded[...], dyn_high[:, cols], preferred_element_type=jnp.float32)
        change = dynamics[:, cols] - sigma_gain * (gain[:, cols] + moved)
        gain[:, cols] = change
        high = change.astype(jnp.bfloat16)
        halves[0, :, cols] = high
        halves[1, :, cols] = (change - high.astype(jnp.float32)).astype(jnp.bfloat16)

    @pl.when(r == 0)
    def _():
        lend.start()

        def settle_sent(k, _):
            settle(columns(k))
            part(0, k).start()
            return 0

        lax.fori_loop(0, tiles, settle_sent, 0)
        for k in range(tiles):
            part(1, k).start()

    @pl.when(r == 1)
    def _():
        def settle_kept(k, _):
            settle(span(k))
            return 0

        lax.fori_loop(0, width // wide, settle_kept, 0)

    lane = lax.broadcasted_iota(jnp.int32, (subs, LANES), 1)
    line = lax.broadcasted_iota(jnp.int32, (subs, LANES), 0)
    group = LANES

    def apply(matrix, vector):
        pieces = [jnp.broadcast_to(vector[k : k + 1, :], (subs, LANES)) for k in range(subs)]

        def rows(step, total):
            for inner in range(group):
                g = step * group + inner
                own = pl.ds(pl.multiple_of(g * subs, subs), subs)
                part = matrix[own, 0:LANES] * pieces[0]
                for k in range(1, subs):
                    part = part + matrix[own, k * LANES : (k + 1) * LANES] * pieces[k]
                total = jnp.where(lane == g, jnp.sum(part, axis=1, keepdims=True), total)
            return total

        total = lax.fori_loop(0, LANES // group, rows, jnp.zeros((subs, LANES), jnp.float32))
        result = jnp.zeros((subs, LANES), jnp.float32)
        for k in range(subs):
            spots = lane // subs + k * (LANES // subs)
            moved = jnp.take_along_axis(total, spots, axis=1)
            kept = jnp.where(line == lax.rem(lane, subs), moved, 0.0)
            result = jnp.where(line == k, jnp.sum(kept, axis=0, keepdims=True), result)
        return result

    @pl.when(r == 0)
    def _():
        lend.wait_send()
        for i in range(2):
            for k in range(tiles):
                part(i, k).wait_send()

    @pl.when(r == 1)
    def _():
        lend.wait_recv()
        b_ref[...] += b_got[...] + apply(gain, b_got[...])
        def compose_high(k, _):
            for inner in range(wide // tile):
                part(0, k * (wide // tile) + inner).wait_recv()
            cols = span(k)
            high = right[0, :, cols]
            whole[:, cols] = (
                gain[:, cols] + high.astype(jnp.float32)
                + jnp.dot(halves[0], high, preferred_element_type=jnp.float32)
                + jnp.dot(halves[1], high, preferred_element_type=jnp.float32)
            )
            return 0

        lax.fori_loop(0, width // wide, compose_high, 0)

        def compose_low(k, _):
            for inner in range(wide // tile):
                part(1, k * (wide // tile) + inner).wait_recv()
            cols = span(k)
            low = right[1, :, cols]
            whole[:, cols] += low.astype(jnp.float32) + jnp.dot(
                halves[0], low, preferred_element_type=jnp.float32
            )
            return 0

        lax.fori_loop(0, width // wide, compose_low, 0)

    onward = push(went, came, pass_send.at[1], pass_recv.at[0], (after, 1))
    aside = push(went, came, pass_send.at[0], pass_recv.at[0], (after, 0))

    @pl.when(place_here == 0)
    def _():
        came[...] = start_ref[...]

    @pl.when(place_here > 0)
    def _():
        onward.wait_recv()

    passing = (r == 1) & (place_here < last)

    @pl.when(r == 1)
    def _():
        state = came[...]
        went[...] = apply(whole, state) + (b_ref[...] + state)

    @pl.when(passing)
    def _():
        onward.start()
        aside.start()

    @pl.when(r == 0)
    def _():
        state = came[...]
        went[...] = apply(gain, state) + (b_ref[...] + state)

    stays = place_here == t

    def report(core, sender):
        return push(
            went, back.at[sender], out_send.at[core], out_recv.at[sender], (place_here, core)
        )

    for core in range(2):
        @pl.when(jnp.logical_not(stays & (r == core)))
        def _():
            report(core, r).start()

        @pl.when(stays & (r == core))
        def _():
            back[core] = went[...]

    for core in range(2):
        @pl.when(jnp.logical_not(stays & (r == core)))
        def _():
            report(core, core).wait_recv()
            report(core, r).wait_send()

    part = subs // 2

    @pl.when(r == 0)
    def _():
        out_ref[0] = back[0, :part, :]
        out_ref[1] = back[1, :part, :]

    @pl.when(r == 1)
    def _():
        out_ref[0] = back[0, part:, :]
        out_ref[1] = back[1, part:, :]

    @pl.when(passing)
    def _():
        onward.wait_send()
        aside.wait_send()

    def finish(slab, _):
        @pl.when(slab != me)
        def _():
            rows, tags = copies(slab, here)
            rows.wait_send()

            @pl.when(r == 0)
            def _():
                tags.wait_send()

        return 0

    lax.fori_loop(0, slabs, finish, 0)


def body(initial, dynamics, obs_rows, obs_values, obs_slab):
    time_devs = lax.axis_size("tm")
    row_devs = lax.axis_size("row")
    width = dynamics.shape[1]
    count, local = obs_rows.shape
    slabs = time_devs * row_devs
    subs = width // LANES
    tiles = width // 256
    vmem = pl.BlockSpec(memory_space=pltpu.VMEM)
    anywhere = pl.BlockSpec(memory_space=pl.ANY)
    small = pltpu.VMEM((subs, LANES), jnp.float32)
    square = pltpu.VMEM((width, width), jnp.float32)
    halves = pltpu.VMEM((2, width, width), jnp.bfloat16)
    sems = pltpu.SemaphoreType.DMA((slabs,))
    states = pl.pallas_call(
        observer_kernel,
        out_shape=jax.ShapeDtypeStruct((2, subs // 2, LANES), jnp.float32),
        in_specs=[vmem, anywhere, vmem, anywhere, vmem],
        out_specs=vmem,
        scratch_shapes=[
            pltpu.VMEM((count, local), jnp.bfloat16),
            pltpu.VMEM((1, count), jnp.float32),
            pltpu.VMEM((slabs, CAP, local), jnp.bfloat16),
            pltpu.VMEM((slabs, 1, LANES), jnp.float32),
            pltpu.VMEM((1, count), jnp.int32),
            pltpu.VMEM((time_devs * CAP, width), jnp.bfloat16),
            pltpu.VMEM((slabs, 1, LANES), jnp.float32),
            square,
            pltpu.VMEM((width, width), jnp.bfloat16),
            pltpu.VMEM((width, 256), jnp.bfloat16),
            pltpu.VMEM((width, width), jnp.bfloat16),
            square,
            pltpu.VMEM((8, width), jnp.float32),
            square,
            halves,
            halves,
            small,
            small,
            small,
            small,
            pltpu.VMEM((2, subs, LANES), jnp.float32),
            sems,
            sems,
            sems,
            sems,
            pltpu.SemaphoreType.DMA((4,)),
            pltpu.SemaphoreType.DMA((2,)),
            pltpu.SemaphoreType.DMA((2, tiles)),
            pltpu.SemaphoreType.DMA((2, tiles)),
            pltpu.SemaphoreType.DMA((2,)),
            pltpu.SemaphoreType.DMA((1,)),
            pltpu.SemaphoreType.DMA((2,)),
            pltpu.SemaphoreType.DMA((2,)),
        ],
        compiler_params=pltpu.CompilerParams(
            collective_id=0, has_side_effects=True, vmem_limit_bytes=60 << 20
        ),
        name="observer",
    )(
        obs_slab.reshape(1, -1),
        obs_rows,
        obs_values.reshape(-1, LANES),
        dynamics,
        initial.reshape(subs, LANES),
    )
    return states.reshape(2, width // 2)


def solution(mesh):
    placed = (P(), P(), P("tm", "row"), P("tm"), P("tm", None))
    return jax.shard_map(
        body, mesh=mesh, in_specs=placed, out_specs=P("tm", "row"), check_vma=False
    )
```

```python
import jax
import jax.numpy as jnp
from jax import lax
from jax.experimental import pallas as pl
from jax.experimental.pallas import tpu as pltpu
from jax.sharding import PartitionSpec as P

CAP = 64
LANES = 128
MESH = pl.DeviceIdType.MESH

sigma_gain = 0.3


def visit(own, turn, total):
    if total & (total - 1):
        return lax.rem(own + turn, total)
    return own ^ turn


def chip_at(place, planes):
    column = place // planes
    depth = lax.rem(place, planes)
    depth = jnp.where(column & 1 == 1, depth, planes - 1 - depth)
    turn = (column + 3) & 3
    return depth * 4 + (turn ^ (turn >> 1))


def place_of(chip, planes):
    depth, turn = chip // 4, chip & 3
    column = ((turn ^ (turn >> 1)) + 1) & 3
    depth = jnp.where(column & 1 == 1, depth, planes - 1 - depth)
    return column * planes + depth


def observer_kernel(
    target_ref, rows_hbm, values_ref, dynamics_ref, start_ref, out_ref,
    rows_ref, values_row, sent, sent_values, slot_ref, got, got_values, dynamics, dyn_high, turned, rounded, gain, moment,
    whole, halves, right, b_ref, b_got, came, went, back,
    all_sent, row_recv, value_recv, own_sem, lend_sem, tile_send, tile_recv, pass_send, pass_recv,
    out_send, out_recv,
):
    time_devs, row_devs = lax.axis_size("tm"), lax.axis_size("row")
    t, r = lax.axis_index("tm"), lax.axis_index("row")
    slabs = time_devs * row_devs
    last = time_devs - 1
    planes = time_devs // 4
    place_here = place_of(t, planes)
    after = chip_at(jnp.minimum(place_here + 1, last), planes)
    me = place_here * row_devs + r
    here = t * row_devs + r
    partner = (t, 1 - r)
    count, local = rows_ref.shape
    width = local * row_devs
    subs = width // LANES
    tile = 256
    tiles = width // tile
    wide = 2 * tile
    block = 256
    share = block // CAP
    blocks = slabs // share

    def device(slab):
        return (chip_at(slab // row_devs, planes), lax.rem(slab, row_devs))

    barrier = pltpu.get_barrier_semaphore()

    def greet(turn, _):
        other = visit(here, slabs - 1 - turn, slabs)
        pl.semaphore_signal(
            barrier, inc=1, device_id=(other // row_devs, lax.rem(other, row_devs)),
            device_id_type=MESH,
        )
        return 0

    lax.fori_loop(0, slabs - 1, greet, 0)
    rows_in = pltpu.make_async_copy(rows_hbm, rows_ref, own_sem.at[1])
    rows_in.start()
    fetch = pltpu.make_async_copy(dynamics_ref, dynamics, own_sem.at[0])
    fetch.start()

    before = (
        lax.broadcasted_iota(jnp.int32, (block, block), 0)
        < lax.broadcasted_iota(jnp.int32, (block, block), 1)
    ).astype(jnp.float32).astype(jnp.bfloat16)
    slab_of = lax.broadcasted_iota(jnp.int32, (slabs, block), 0)
    carry = (slab_of[:, :1] * CAP).astype(jnp.float32)
    for start in range(0, count, block):
        named = (target_ref[:, start : start + block] == slab_of).astype(jnp.float32)
        ahead = jnp.dot(named.astype(jnp.bfloat16), before, preferred_element_type=jnp.float32)
        slot = jnp.sum(named * (ahead + carry), axis=0, keepdims=True)
        slot_ref[:, start : start + block] = slot.astype(jnp.int32)
        carry = carry + jnp.sum(named, axis=1, keepdims=True)

    spread = values_ref[...].astype(jnp.float32)
    for line in range(count // LANES):
        values_row[:, line * LANES : (line + 1) * LANES] = spread[line : line + 1, :]
    values = jnp.broadcast_to(values_row[...], (8, count)).astype(jnp.bfloat16)
    sent_values[...] = jnp.zeros_like(sent_values)

    def landing(source):
        rows = pl.ds(pl.multiple_of(source // row_devs * CAP, CAP), CAP)
        cols = pl.ds(pl.multiple_of(lax.rem(source, row_devs) * local, local), local)
        return got.at[rows, cols]

    chips = block // CAP
    groups = time_devs // chips
    nearest = t // chips

    def copies(slab):
        rows = pltpu.make_async_remote_copy(
            src_ref=sent.at[slab], dst_ref=landing(here),
            send_sem=all_sent.at[0], recv_sem=row_recv.at[nearest],
            device_id=device(slab), device_id_type=MESH,
        )
        tags = pltpu.make_async_remote_copy(
            src_ref=sent_values.at[slab], dst_ref=got_values.at[t],
            send_sem=all_sent.at[1], recv_sem=value_recv.at[nearest],
            device_id=device(slab), device_id_type=MESH,
        )
        return rows, tags

    keep = (
        pltpu.make_async_copy(sent.at[me], landing(here), row_recv.at[nearest]),
        pltpu.make_async_copy(sent_values.at[me], got_values.at[t], value_recv.at[nearest]),
    )

    def place(at):
        first = at * share
        wanted = lax.broadcasted_iota(jnp.int32, (block, count), 0) + first * CAP
        pick = (wanted == slot_ref[...]).astype(jnp.float32).astype(jnp.bfloat16)
        rows = jnp.dot(pick, rows_ref[...], preferred_element_type=jnp.float32).astype(jnp.bfloat16)
        tags = lax.dot_general(
            values, pick, (((1,), (1,)), ((), ())), preferred_element_type=jnp.float32
        )[:1]
        for inner in range(share):
            sent[first + inner] = rows[inner * CAP : (inner + 1) * CAP]
            sent_values[first + inner, :, :CAP] = tags[:, inner * CAP : (inner + 1) * CAP]

    column_blocks = planes * row_devs // share
    depth = t // 4

    def order(turn):
        mixed = lax.rem(turn, 2) * column_blocks + turn // 2
        turn = jnp.where(((t >> 1) & 1 == 0) & (turn < 2 * column_blocks), mixed, turn)
        column = turn // column_blocks
        along = jnp.where(column & 1 == 1, depth, planes - 1 - depth)
        own = along * row_devs // share
        return column * column_blocks + (own ^ lax.rem(turn, column_blocks)), along

    def send(turn):
        at, along = order(turn)
        key = lax.rem(along * row_devs, share) + r
        for inner in range(share):
            slab = at * share + (key ^ inner)

            @pl.when(slab != me)
            def _():
                rows, tags = copies(slab)
                rows.start()

                @pl.when(r == 0)
                def _():
                    tags.start()

            @pl.when(slab == me)
            def _():
                keep[0].start()

                @pl.when(r == 0)
                def _():
                    keep[1].start()

    rows_in.wait()
    place(order(0)[0])
    pl.semaphore_wait(barrier, slabs - 1)
    send(0)

    def step(turn, _):
        place(order(turn)[0])
        send(turn)
        return 0

    lax.fori_loop(1, blocks, step, 0)

    fetch.wait()

    def divide(k, _):
        rows = pl.ds(pl.multiple_of(k * LANES, LANES), LANES)
        high = dynamics[rows, :].astype(jnp.bfloat16)
        dyn_high[rows, :] = high
        return 0

    lax.fori_loop(0, subs, divide, 0)
    gain[...] = jnp.zeros_like(gain)
    moment[...] = jnp.zeros_like(moment)

    def gather(turn, _):
        at = visit(nearest, turn, groups)
        own = pl.ds(pl.multiple_of(at * block, block), block)
        named = pl.ds(at * chips, chips)
        pltpu.make_async_copy(got.at[own], got.at[own], row_recv.at[at]).wait()
        pltpu.make_async_copy(got_values.at[named], got_values.at[named], value_recv.at[at]).wait()
        rows = got[own, :]
        turned[...] = rows.T
        tags = jnp.concatenate(
            [got_values[at * chips + k][:, :CAP] for k in range(chips)], axis=1
        )
        tags = jnp.broadcast_to(tags, (8, block)).astype(jnp.bfloat16)
        moment[...] += jnp.dot(tags, rows, preferred_element_type=jnp.float32)

        def column(k, _):
            cols = pl.ds(pl.multiple_of(k * wide, wide), wide)
            gain[:, cols] += jnp.dot(turned[...], got[own, cols], preferred_element_type=jnp.float32)
            return 0

        lax.fori_loop(0, width // wide, column, 0)
        return 0

    lax.fori_loop(0, groups, gather, 0)

    def push(source, target, send_sem, recv_sem, peer):
        return pltpu.make_async_remote_copy(
            src_ref=source, dst_ref=target, send_sem=send_sem, recv_sem=recv_sem,
            device_id=peer, device_id_type=MESH,
        )

    lend = push(b_ref, b_got, lend_sem.at[0], lend_sem.at[1], partner)

    def columns(k):
        return pl.ds(pl.multiple_of(k * tile, tile), tile)

    def part(i, k):
        cols = columns(k)
        return push(
            halves.at[i, :, cols], right.at[i, :, cols], tile_send, tile_recv.at[i, k // 2], partner,
        )

    for sub in range(subs):
        b_ref[sub : sub + 1, :] = sigma_gain * moment[:1, sub * LANES : (sub + 1) * LANES]

    for k in range(tiles):
        rows = slice(k * tile, (k + 1) * tile)
        rounded[rows, :] = gain[rows, :].astype(jnp.bfloat16)

    def span(k):
        return pl.ds(pl.multiple_of(k * wide, wide), wide)

    def settle(cols):
        moved = jnp.dot(rounded[...], dyn_high[:, cols], preferred_element_type=jnp.float32)
        change = dynamics[:, cols] - sigma_gain * (gain[:, cols] + moved)
        gain[:, cols] = change
        high = change.astype(jnp.bfloat16)
        halves[0, :, cols] = high
        halves[1, :, cols] = (change - high.astype(jnp.float32)).astype(jnp.bfloat16)

    @pl.when(r == 0)
    def _():
        lend.start()

        def settle_sent(k, _):
            settle(columns(k))
            part(0, k).start()
            return 0

        lax.fori_loop(0, tiles, settle_sent, 0)
        for k in range(tiles):
            part(1, k).start()

    @pl.when(r == 1)
    def _():
        def settle_kept(k, _):
            settle(span(k))
            return 0

        lax.fori_loop(0, width // wide, settle_kept, 0)

    lane = lax.broadcasted_iota(jnp.int32, (subs, LANES), 1)
    line = lax.broadcasted_iota(jnp.int32, (subs, LANES), 0)
    group = LANES

    def apply(matrix, vector):
        pieces = [jnp.broadcast_to(vector[k : k + 1, :], (subs, LANES)) for k in range(subs)]

        def rows(step, total):
            for inner in range(group):
                g = step * group + inner
                own = pl.ds(pl.multiple_of(g * subs, subs), subs)
                part = matrix[own, 0:LANES] * pieces[0]
                for k in range(1, subs):
                    part = part + matrix[own, k * LANES : (k + 1) * LANES] * pieces[k]
                total = jnp.where(lane == g, jnp.sum(part, axis=1, keepdims=True), total)
            return total

        total = lax.fori_loop(0, LANES // group, rows, jnp.zeros((subs, LANES), jnp.float32))
        result = jnp.zeros((subs, LANES), jnp.float32)
        for k in range(subs):
            spots = lane // subs + k * (LANES // subs)
            moved = jnp.take_along_axis(total, spots, axis=1)
            kept = jnp.where(line == lax.rem(lane, subs), moved, 0.0)
            result = jnp.where(line == k, jnp.sum(kept, axis=0, keepdims=True), result)
        return result

    @pl.when(r == 0)
    def _():
        lend.wait_send()
        push(halves, right, tile_send, tile_recv.at[0, 0], partner).wait_send()

    @pl.when(r == 1)
    def _():
        lend.wait_recv()
        b_ref[...] += b_got[...] + apply(gain, b_got[...])
        def compose_high(k, _):
            cols = span(k)
            pltpu.make_async_copy(
                right.at[0, :, cols], right.at[0, :, cols], tile_recv.at[0, k]
            ).wait()
            high = right[0, :, cols]
            whole[:, cols] = (
                gain[:, cols] + high.astype(jnp.float32)
                + jnp.dot(halves[0], high, preferred_element_type=jnp.float32)
                + jnp.dot(halves[1], high, preferred_element_type=jnp.float32)
            )
            return 0

        lax.fori_loop(0, width // wide, compose_high, 0)

        def compose_low(k, _):
            cols = span(k)
            pltpu.make_async_copy(
                right.at[1, :, cols], right.at[1, :, cols], tile_recv.at[1, k]
            ).wait()
            low = right[1, :, cols]
            whole[:, cols] += low.astype(jnp.float32) + jnp.dot(
                halves[0], low, preferred_element_type=jnp.float32
            )
            return 0

        lax.fori_loop(0, width // wide, compose_low, 0)

    onward = push(went, came, pass_send.at[1], pass_recv.at[0], (after, 1))
    aside = push(went, came, pass_send.at[0], pass_recv.at[0], (after, 0))

    @pl.when(place_here == 0)
    def _():
        came[...] = start_ref[...]

    @pl.when(place_here > 0)
    def _():
        onward.wait_recv()

    passing = (r == 1) & (place_here < last)

    @pl.when(r == 1)
    def _():
        state = came[...]
        went[...] = apply(whole, state) + (b_ref[...] + state)

    @pl.when(passing)
    def _():
        onward.start()
        aside.start()

    @pl.when(r == 0)
    def _():
        state = came[...]
        went[...] = apply(gain, state) + (b_ref[...] + state)

    stays = place_here == t

    def report(core, sender):
        return push(
            went, back.at[sender], out_send.at[core], out_recv.at[sender], (place_here, core)
        )

    for core in range(2):
        @pl.when(jnp.logical_not(stays & (r == core)))
        def _():
            report(core, r).start()

        @pl.when(stays & (r == core))
        def _():
            back[core] = went[...]

    for core in range(2):
        @pl.when(jnp.logical_not(stays & (r == core)))
        def _():
            report(core, core).wait_recv()
            report(core, r).wait_send()

    part = subs // 2

    @pl.when(r == 0)
    def _():
        out_ref[0] = back[0, :part, :]
        out_ref[1] = back[1, :part, :]

    @pl.when(r == 1)
    def _():
        out_ref[0] = back[0, part:, :]
        out_ref[1] = back[1, part:, :]

    @pl.when(passing)
    def _():
        onward.wait_send()
        aside.wait_send()

    pltpu.make_async_copy(
        sent.at[pl.ds(0, slabs - 1)], sent.at[pl.ds(0, slabs - 1)], all_sent.at[0]
    ).wait()

    @pl.when(r == 0)
    def _():
        pltpu.make_async_copy(
            sent_values.at[pl.ds(0, slabs - 1)], sent_values.at[pl.ds(0, slabs - 1)], all_sent.at[1]
        ).wait()


def body(initial, dynamics, obs_rows, obs_values, obs_slab):
    time_devs = lax.axis_size("tm")
    row_devs = lax.axis_size("row")
    width = dynamics.shape[1]
    count, local = obs_rows.shape
    slabs = time_devs * row_devs
    subs = width // LANES
    tiles = width // 256
    vmem = pl.BlockSpec(memory_space=pltpu.VMEM)
    anywhere = pl.BlockSpec(memory_space=pl.ANY)
    small = pltpu.VMEM((subs, LANES), jnp.float32)
    square = pltpu.VMEM((width, width), jnp.float32)
    halves = pltpu.VMEM((2, width, width), jnp.bfloat16)
    sems = pltpu.SemaphoreType.DMA((time_devs * CAP // 256,))
    states = pl.pallas_call(
        observer_kernel,
        out_shape=jax.ShapeDtypeStruct((2, subs // 2, LANES), jnp.float32),
        in_specs=[vmem, anywhere, vmem, anywhere, vmem],
        out_specs=vmem,
        scratch_shapes=[
            pltpu.VMEM((count, local), jnp.bfloat16),
            pltpu.VMEM((1, count), jnp.float32),
            pltpu.VMEM((slabs, CAP, local), jnp.bfloat16),
            pltpu.VMEM((slabs, 1, LANES), jnp.float32),
            pltpu.VMEM((1, count), jnp.int32),
            pltpu.VMEM((time_devs * CAP, width), jnp.bfloat16),
            pltpu.VMEM((time_devs, 1, LANES), jnp.float32),
            square,
            pltpu.VMEM((width, width), jnp.bfloat16),
            pltpu.VMEM((width, 256), jnp.bfloat16),
            pltpu.VMEM((width, width), jnp.bfloat16),
            square,
            pltpu.VMEM((8, width), jnp.float32),
            square,
            halves,
            halves,
            small,
            small,
            small,
            small,
            pltpu.VMEM((2, subs, LANES), jnp.float32),
            pltpu.SemaphoreType.DMA((2,)),
            sems,
            sems,
            pltpu.SemaphoreType.DMA((2,)),
            pltpu.SemaphoreType.DMA((2,)),
            pltpu.SemaphoreType.DMA,
            pltpu.SemaphoreType.DMA((2, tiles // 2)),
            pltpu.SemaphoreType.DMA((2,)),
            pltpu.SemaphoreType.DMA((1,)),
            pltpu.SemaphoreType.DMA((2,)),
            pltpu.SemaphoreType.DMA((2,)),
        ],
        compiler_params=pltpu.CompilerParams(
            collective_id=0, has_side_effects=True, vmem_limit_bytes=60 << 20
        ),
        name="observer",
    )(
        obs_slab.reshape(1, -1),
        obs_rows,
        obs_values.reshape(-1, LANES),
        dynamics,
        initial.reshape(subs, LANES),
    )
    return states.reshape(2, width // 2)


def solution(mesh):
    placed = (P(), P(), P("tm", "row"), P("tm"), P("tm", None))
    return jax.shard_map(
        body, mesh=mesh, in_specs=placed, out_specs=P("tm", "row"), check_vma=False
    )
```

```python
import jax
import jax.numpy as jnp
from jax import lax
from jax.experimental import pallas as pl
from jax.experimental.pallas import tpu as pltpu
from jax.sharding import PartitionSpec as P

CAP = 64
LANES = 128
MESH = pl.DeviceIdType.MESH

sigma_gain = 0.3


def visit(own, turn, total):
    if total & (total - 1):
        return lax.rem(own + turn, total)
    return own ^ turn


def chip_at(place, planes):
    column = place // planes
    depth = lax.rem(place, planes)
    depth = jnp.where(column & 1 == 1, depth, planes - 1 - depth)
    turn = (column + 3) & 3
    return depth * 4 + (turn ^ (turn >> 1))


def place_of(chip, planes):
    depth, turn = chip // 4, chip & 3
    column = ((turn ^ (turn >> 1)) + 1) & 3
    depth = jnp.where(column & 1 == 1, depth, planes - 1 - depth)
    return column * planes + depth


def observer_kernel(
    target_ref, rows_hbm, values_ref, dynamics_ref, start_ref, out_ref,
    rows_ref, values_row, sent, sent_values, slot_ref, got, got_values, dynamics, dyn_high, turned, rounded, gain, moment,
    whole, halves, right, b_ref, b_got, came, went, back,
    all_sent, row_recv, value_recv, own_sem, lend_sem, tile_send, tile_recv, pass_send, pass_recv,
    out_send, out_recv,
):
    time_devs, row_devs = lax.axis_size("tm"), lax.axis_size("row")
    t, r = lax.axis_index("tm"), lax.axis_index("row")
    slabs = time_devs * row_devs
    last = time_devs - 1
    planes = time_devs // 4
    place_here = place_of(t, planes)
    after = chip_at(jnp.minimum(place_here + 1, last), planes)
    me = place_here * row_devs + r
    here = t * row_devs + r
    partner = (t, 1 - r)
    count, local = rows_ref.shape
    width = local * row_devs
    subs = width // LANES
    tile = 256
    tiles = width // tile
    wide = 2 * tile
    block = 256
    share = block // CAP
    blocks = slabs // share

    def device(slab):
        return (chip_at(slab // row_devs, planes), lax.rem(slab, row_devs))

    barrier = pltpu.get_barrier_semaphore()

    def greet(turn, _):
        other = visit(here, slabs - 1 - turn, slabs)
        pl.semaphore_signal(
            barrier, inc=1, device_id=(other // row_devs, lax.rem(other, row_devs)),
            device_id_type=MESH,
        )
        return 0

    lax.fori_loop(0, slabs - 1, greet, 0)
    rows_in = pltpu.make_async_copy(rows_hbm, rows_ref, own_sem.at[1])
    rows_in.start()
    fetch = pltpu.make_async_copy(dynamics_ref, dynamics, own_sem.at[0])
    fetch.start()

    before = (
        lax.broadcasted_iota(jnp.int32, (block, block), 0)
        < lax.broadcasted_iota(jnp.int32, (block, block), 1)
    ).astype(jnp.float32).astype(jnp.bfloat16)
    slab_of = lax.broadcasted_iota(jnp.int32, (slabs, block), 0)
    carry = (slab_of[:, :1] * CAP).astype(jnp.float32)
    for start in range(0, count, block):
        named = (target_ref[:, start : start + block] == slab_of).astype(jnp.float32)
        ahead = jnp.dot(named.astype(jnp.bfloat16), before, preferred_element_type=jnp.float32)
        slot = jnp.sum(named * (ahead + carry), axis=0, keepdims=True)
        slot_ref[:, start : start + block] = slot.astype(jnp.int32)
        carry = carry + jnp.sum(named, axis=1, keepdims=True)

    spread = values_ref[...].astype(jnp.float32)
    for line in range(count // LANES):
        values_row[:, line * LANES : (line + 1) * LANES] = spread[line : line + 1, :]
    values = jnp.broadcast_to(values_row[...], (8, count)).astype(jnp.bfloat16)
    sent_values[...] = jnp.zeros_like(sent_values)

    def landing(source):
        rows = pl.ds(pl.multiple_of(source // row_devs * CAP, CAP), CAP)
        cols = pl.ds(pl.multiple_of(lax.rem(source, row_devs) * local, local), local)
        return got.at[rows, cols]

    chips = block // CAP
    groups = time_devs // chips
    nearest = t // chips

    def copies(slab):
        rows = pltpu.make_async_remote_copy(
            src_ref=sent.at[slab], dst_ref=landing(here),
            send_sem=all_sent.at[0], recv_sem=row_recv.at[nearest],
            device_id=device(slab), device_id_type=MESH,
        )
        tags = pltpu.make_async_remote_copy(
            src_ref=sent_values.at[slab], dst_ref=got_values.at[t],
            send_sem=all_sent.at[1], recv_sem=value_recv.at[nearest],
            device_id=device(slab), device_id_type=MESH,
        )
        return rows, tags

    keep = (
        pltpu.make_async_copy(sent.at[me], landing(here), row_recv.at[nearest]),
        pltpu.make_async_copy(sent_values.at[me], got_values.at[t], value_recv.at[nearest]),
    )

    def place(at):
        first = at * share
        wanted = lax.broadcasted_iota(jnp.int32, (block, count), 0) + first * CAP
        pick = (wanted == slot_ref[...]).astype(jnp.float32).astype(jnp.bfloat16)
        rows = jnp.dot(pick, rows_ref[...], preferred_element_type=jnp.float32).astype(jnp.bfloat16)
        tags = lax.dot_general(
            values, pick, (((1,), (1,)), ((), ())), preferred_element_type=jnp.float32
        )[:1]
        for inner in range(share):
            sent[first + inner] = rows[inner * CAP : (inner + 1) * CAP]
            sent_values[first + inner, :, :CAP] = tags[:, inner * CAP : (inner + 1) * CAP]

    column_blocks = planes * row_devs // share
    depth = t // 4

    def order(turn):
        mixed = lax.rem(turn, 2) * column_blocks + turn // 2
        turn = jnp.where(((t >> 1) & 1 == 0) & (turn < 2 * column_blocks), mixed, turn)
        column = turn // column_blocks
        along = jnp.where(column & 1 == 1, depth, planes - 1 - depth)
        own = along * row_devs // share
        return column * column_blocks + (own ^ lax.rem(turn, column_blocks)), along

    def send(turn):
        at, along = order(turn)
        key = lax.rem(along * row_devs, share) + r
        for inner in range(share):
            slab = at * share + (key ^ inner)

            @pl.when(slab != me)
            def _():
                rows, tags = copies(slab)
                rows.start()

                @pl.when(r == 0)
                def _():
                    tags.start()

            @pl.when(slab == me)
            def _():
                keep[0].start()

                @pl.when(r == 0)
                def _():
                    keep[1].start()

    rows_in.wait()
    place(order(0)[0])
    pl.semaphore_wait(barrier, slabs - 1)
    send(0)

    def step(turn, _):
        place(order(turn)[0])
        send(turn)
        return 0

    lax.fori_loop(1, blocks, step, 0)

    fetch.wait()

    def divide(k, _):
        rows = pl.ds(pl.multiple_of(k * LANES, LANES), LANES)
        high = dynamics[rows, :].astype(jnp.bfloat16)
        dyn_high[rows, :] = high
        return 0

    lax.fori_loop(0, subs, divide, 0)
    gain[...] = jnp.zeros_like(gain)
    moment[...] = jnp.zeros_like(moment)

    def gather(turn, _):
        at = visit(nearest, turn, groups)
        own = pl.ds(pl.multiple_of(at * block, block), block)
        named = pl.ds(at * chips, chips)
        pltpu.make_async_copy(got.at[own], got.at[own], row_recv.at[at]).wait()
        pltpu.make_async_copy(got_values.at[named], got_values.at[named], value_recv.at[at]).wait()
        rows = got[own, :]
        turned[...] = rows.T
        tags = jnp.concatenate(
            [got_values[at * chips + k][:, :CAP] for k in range(chips)], axis=1
        )
        tags = jnp.broadcast_to(tags, (8, block)).astype(jnp.bfloat16)
        moment[...] += jnp.dot(tags, rows, preferred_element_type=jnp.float32)

        def column(k, _):
            cols = pl.ds(pl.multiple_of(k * wide, wide), wide)
            gain[:, cols] += jnp.dot(turned[...], got[own, cols], preferred_element_type=jnp.float32)
            return 0

        lax.fori_loop(0, width // wide, column, 0)
        return 0

    lax.fori_loop(0, groups, gather, 0)

    def push(source, target, send_sem, recv_sem, peer):
        return pltpu.make_async_remote_copy(
            src_ref=source, dst_ref=target, send_sem=send_sem, recv_sem=recv_sem,
            device_id=peer, device_id_type=MESH,
        )

    lend = push(b_ref, b_got, lend_sem.at[0], lend_sem.at[1], partner)

    def columns(k):
        return pl.ds(pl.multiple_of(k * tile, tile), tile)

    def part(i, k):
        cols = columns(k)
        source = right if i else halves
        return push(
            source.at[i, :, cols], right.at[i, :, cols], tile_send,
            tile_recv.at[i, k if i else k // 2], partner,
        )

    for sub in range(subs):
        b_ref[sub : sub + 1, :] = sigma_gain * moment[:1, sub * LANES : (sub + 1) * LANES]

    for k in range(tiles):
        rows = slice(k * tile, (k + 1) * tile)
        rounded[rows, :] = gain[rows, :].astype(jnp.bfloat16)

    def span(k):
        return pl.ds(pl.multiple_of(k * wide, wide), wide)

    spans = width // wide

    def give(k):
        cols = span(k)
        return push(
            halves.at[0, :, cols], right.at[0, :, cols], tile_send, tile_recv.at[0, k], partner
        )

    def settle(cols):
        moved = jnp.dot(rounded[...], dyn_high[:, cols], preferred_element_type=jnp.float32)
        change = dynamics[:, cols] - sigma_gain * (gain[:, cols] + moved)
        gain[:, cols] = change
        high = change.astype(jnp.bfloat16)
        halves[0, :, cols] = high
        halves[1, :, cols] = (change - high.astype(jnp.float32)).astype(jnp.bfloat16)

    @pl.when(r == 0)
    def _():
        lend.start()

        def settle_sent(k, _):
            settle(columns(k))
            part(0, k).start()
            return 0

        lax.fori_loop(0, tiles, settle_sent, 0)

    @pl.when(r == 1)
    def _():
        def settle_kept(k, _):
            settle(span(k))
            give(k).start()
            return 0

        lax.fori_loop(0, spans, settle_kept, 0)

    lane = lax.broadcasted_iota(jnp.int32, (subs, LANES), 1)
    line = lax.broadcasted_iota(jnp.int32, (subs, LANES), 0)
    group = LANES

    def apply(matrix, vector):
        pieces = [jnp.broadcast_to(vector[k : k + 1, :], (subs, LANES)) for k in range(subs)]

        def rows(step, total):
            for inner in range(group):
                g = step * group + inner
                own = pl.ds(pl.multiple_of(g * subs, subs), subs)
                part = matrix[own, 0:LANES] * pieces[0]
                for k in range(1, subs):
                    part = part + matrix[own, k * LANES : (k + 1) * LANES] * pieces[k]
                total = jnp.where(lane == g, jnp.sum(part, axis=1, keepdims=True), total)
            return total

        total = lax.fori_loop(0, LANES // group, rows, jnp.zeros((subs, LANES), jnp.float32))
        result = jnp.zeros((subs, LANES), jnp.float32)
        for k in range(subs):
            spots = lane // subs + k * (LANES // subs)
            moved = jnp.take_along_axis(total, spots, axis=1)
            kept = jnp.where(line == lax.rem(lane, subs), moved, 0.0)
            result = jnp.where(line == k, jnp.sum(kept, axis=0, keepdims=True), result)
        return result

    @pl.when(r == 0)
    def _():
        def refine(j, cols):
            deep = span(j)
            return jnp.dot(
                right[0, :, deep], halves[1, deep, cols], preferred_element_type=jnp.float32
            )

        for j in range(spans - 1):
            give(j).wait_recv()

            def early(k, _):
                cols = span(k)
                known = halves[1, :, cols].astype(jnp.float32) if j == 0 else whole[:, cols]
                whole[:, cols] = known + refine(j, cols)
                return 0

            lax.fori_loop(0, spans, early, 0)

        give(spans - 1).wait_recv()

        def late(k, _):
            cols = columns(k)
            right[1, :, cols] = (whole[:, cols] + refine(spans - 1, cols)).astype(jnp.bfloat16)
            part(1, k).start()
            return 0

        lax.fori_loop(0, tiles, late, 0)
        lend.wait_send()
        push(halves, right, tile_send, tile_recv.at[0, 0], partner).wait_send()

    @pl.when(r == 1)
    def _():
        lend.wait_recv()
        b_ref[...] += b_got[...] + apply(gain, b_got[...])
        def compose_high(k, _):
            cols = span(k)
            pltpu.make_async_copy(
                right.at[0, :, cols], right.at[0, :, cols], tile_recv.at[0, k]
            ).wait()
            high = right[0, :, cols]
            whole[:, cols] = (
                gain[:, cols] + high.astype(jnp.float32)
                + jnp.dot(halves[0], high, preferred_element_type=jnp.float32)
                + jnp.dot(halves[1], high, preferred_element_type=jnp.float32)
            )
            return 0

        lax.fori_loop(0, spans, compose_high, 0)

        def compose_low(k, _):
            cols = columns(k)
            part(1, k).wait_recv()
            whole[:, cols] += right[1, :, cols].astype(jnp.float32)
            return 0

        lax.fori_loop(0, tiles, compose_low, 0)
        push(halves.at[0], right.at[0], tile_send, tile_recv.at[0, 0], partner).wait_send()

    onward = push(went, came, pass_send.at[1], pass_recv.at[0], (after, 1))
    aside = push(went, came, pass_send.at[0], pass_recv.at[0], (after, 0))

    @pl.when(place_here == 0)
    def _():
        came[...] = start_ref[...]

    @pl.when(place_here > 0)
    def _():
        onward.wait_recv()

    passing = (r == 1) & (place_here < last)

    @pl.when(r == 1)
    def _():
        state = came[...]
        went[...] = apply(whole, state) + (b_ref[...] + state)

    @pl.when(passing)
    def _():
        onward.start()
        aside.start()

    @pl.when(r == 0)
    def _():
        state = came[...]
        went[...] = apply(gain, state) + (b_ref[...] + state)

    stays = place_here == t

    def report(core, sender):
        return push(
            went, back.at[sender], out_send.at[core], out_recv.at[sender], (place_here, core)
        )

    for core in range(2):
        @pl.when(jnp.logical_not(stays & (r == core)))
        def _():
            report(core, r).start()

        @pl.when(stays & (r == core))
        def _():
            back[core] = went[...]

    for core in range(2):
        @pl.when(jnp.logical_not(stays & (r == core)))
        def _():
            report(core, core).wait_recv()
            report(core, r).wait_send()

    part = subs // 2

    @pl.when(r == 0)
    def _():
        out_ref[0] = back[0, :part, :]
        out_ref[1] = back[1, :part, :]

    @pl.when(r == 1)
    def _():
        out_ref[0] = back[0, part:, :]
        out_ref[1] = back[1, part:, :]

    @pl.when(passing)
    def _():
        onward.wait_send()
        aside.wait_send()

    pltpu.make_async_copy(
        sent.at[pl.ds(0, slabs - 1)], sent.at[pl.ds(0, slabs - 1)], all_sent.at[0]
    ).wait()

    @pl.when(r == 0)
    def _():
        pltpu.make_async_copy(
            sent_values.at[pl.ds(0, slabs - 1)], sent_values.at[pl.ds(0, slabs - 1)], all_sent.at[1]
        ).wait()


def body(initial, dynamics, obs_rows, obs_values, obs_slab):
    time_devs = lax.axis_size("tm")
    row_devs = lax.axis_size("row")
    width = dynamics.shape[1]
    count, local = obs_rows.shape
    slabs = time_devs * row_devs
    subs = width // LANES
    tiles = width // 256
    vmem = pl.BlockSpec(memory_space=pltpu.VMEM)
    anywhere = pl.BlockSpec(memory_space=pl.ANY)
    small = pltpu.VMEM((subs, LANES), jnp.float32)
    square = pltpu.VMEM((width, width), jnp.float32)
    halves = pltpu.VMEM((2, width, width), jnp.bfloat16)
    sems = pltpu.SemaphoreType.DMA((time_devs * CAP // 256,))
    states = pl.pallas_call(
        observer_kernel,
        out_shape=jax.ShapeDtypeStruct((2, subs // 2, LANES), jnp.float32),
        in_specs=[vmem, anywhere, vmem, anywhere, vmem],
        out_specs=vmem,
        scratch_shapes=[
            pltpu.VMEM((count, local), jnp.bfloat16),
            pltpu.VMEM((1, count), jnp.float32),
            pltpu.VMEM((slabs, CAP, local), jnp.bfloat16),
            pltpu.VMEM((slabs, 1, LANES), jnp.float32),
            pltpu.VMEM((1, count), jnp.int32),
            pltpu.VMEM((time_devs * CAP, width), jnp.bfloat16),
            pltpu.VMEM((time_devs, 1, LANES), jnp.float32),
            square,
            pltpu.VMEM((width, width), jnp.bfloat16),
            pltpu.VMEM((width, 256), jnp.bfloat16),
            pltpu.VMEM((width, width), jnp.bfloat16),
            square,
            pltpu.VMEM((8, width), jnp.float32),
            square,
            halves,
            halves,
            small,
            small,
            small,
            small,
            pltpu.VMEM((2, subs, LANES), jnp.float32),
            pltpu.SemaphoreType.DMA((2,)),
            sems,
            sems,
            pltpu.SemaphoreType.DMA((2,)),
            pltpu.SemaphoreType.DMA((2,)),
            pltpu.SemaphoreType.DMA,
            pltpu.SemaphoreType.DMA((2, tiles)),
            pltpu.SemaphoreType.DMA((2,)),
            pltpu.SemaphoreType.DMA((1,)),
            pltpu.SemaphoreType.DMA((2,)),
            pltpu.SemaphoreType.DMA((2,)),
        ],
        compiler_params=pltpu.CompilerParams(
            collective_id=0, has_side_effects=True, vmem_limit_bytes=60 << 20
        ),
        name="observer",
    )(
        obs_slab.reshape(1, -1),
        obs_rows,
        obs_values.reshape(-1, LANES),
        dynamics,
        initial.reshape(subs, LANES),
    )
    return states.reshape(2, width // 2)


def solution(mesh):
    placed = (P(), P(), P("tm", "row"), P("tm"), P("tm", None))
    return jax.shard_map(
        body, mesh=mesh, in_specs=placed, out_specs=P("tm", "row"), check_vma=False
    )
```

```python
import jax
import jax.numpy as jnp
from jax import lax
from jax.experimental import pallas as pl
from jax.experimental.pallas import tpu as pltpu
from jax.sharding import PartitionSpec as P

CAP = 64
LANES = 128
MESH = pl.DeviceIdType.MESH

sigma_gain = 0.3


def visit(own, turn, total):
    if total & (total - 1):
        return lax.rem(own + turn, total)
    return own ^ turn


def chip_at(place, planes):
    column = place // planes
    depth = lax.rem(place, planes)
    depth = jnp.where(column & 1 == 1, depth, planes - 1 - depth)
    turn = (column + 3) & 3
    return depth * 4 + (turn ^ (turn >> 1))


def place_of(chip, planes):
    depth, turn = chip // 4, chip & 3
    column = ((turn ^ (turn >> 1)) + 1) & 3
    depth = jnp.where(column & 1 == 1, depth, planes - 1 - depth)
    return column * planes + depth


def observer_kernel(
    target_ref, rows_hbm, values_ref, dynamics_ref, start_ref, out_ref,
    rows_ref, values_row, sent, sent_values, slot_ref, got, got_values, dynamics, dyn_high, turned, rounded, gain, moment,
    whole, halves, right, b_ref, b_got, came, went, back,
    all_sent, row_recv, value_recv, own_sem, lend_sem, tile_send, tile_recv, pass_send, pass_recv,
    out_send, out_recv,
):
    time_devs, row_devs = lax.axis_size("tm"), lax.axis_size("row")
    t, r = lax.axis_index("tm"), lax.axis_index("row")
    slabs = time_devs * row_devs
    last = time_devs - 1
    planes = time_devs // 4
    place_here = place_of(t, planes)
    after = chip_at(jnp.minimum(place_here + 1, last), planes)
    me = place_here * row_devs + r
    here = t * row_devs + r
    partner = (t, 1 - r)
    count, local = rows_ref.shape
    width = local * row_devs
    subs = width // LANES
    tile = 256
    tiles = width // tile
    wide = 2 * tile
    block = 256
    share = block // CAP
    blocks = slabs // share

    def device(slab):
        return (chip_at(slab // row_devs, planes), lax.rem(slab, row_devs))

    barrier = pltpu.get_barrier_semaphore()

    def greet(turn, _):
        other = visit(here, slabs - 1 - turn, slabs)
        pl.semaphore_signal(
            barrier, inc=1, device_id=(other // row_devs, lax.rem(other, row_devs)),
            device_id_type=MESH,
        )
        return 0

    lax.fori_loop(0, slabs - 1, greet, 0)
    rows_in = pltpu.make_async_copy(rows_hbm, rows_ref, own_sem.at[1])
    rows_in.start()
    fetch = pltpu.make_async_copy(dynamics_ref, dynamics, own_sem.at[0])
    fetch.start()

    before = (
        lax.broadcasted_iota(jnp.int32, (block, block), 0)
        < lax.broadcasted_iota(jnp.int32, (block, block), 1)
    ).astype(jnp.float32).astype(jnp.bfloat16)
    slab_of = lax.broadcasted_iota(jnp.int32, (slabs, block), 0)
    carry = (slab_of[:, :1] * CAP).astype(jnp.float32)
    for start in range(0, count, block):
        named = (target_ref[:, start : start + block] == slab_of).astype(jnp.float32)
        ahead = jnp.dot(named.astype(jnp.bfloat16), before, preferred_element_type=jnp.float32)
        slot = jnp.sum(named * (ahead + carry), axis=0, keepdims=True)
        slot_ref[:, start : start + block] = slot.astype(jnp.int32)
        carry = carry + jnp.sum(named, axis=1, keepdims=True)

    spread = values_ref[...].astype(jnp.float32)
    for line in range(count // LANES):
        values_row[:, line * LANES : (line + 1) * LANES] = spread[line : line + 1, :]
    values = jnp.broadcast_to(values_row[...], (8, count)).astype(jnp.bfloat16)
    sent_values[...] = jnp.zeros_like(sent_values)

    def landing(source):
        rows = pl.ds(pl.multiple_of(source // row_devs * CAP, CAP), CAP)
        cols = pl.ds(pl.multiple_of(lax.rem(source, row_devs) * local, local), local)
        return got.at[rows, cols]

    chips = block // CAP
    groups = time_devs // chips
    nearest = t // chips

    def copies(slab):
        rows = pltpu.make_async_remote_copy(
            src_ref=sent.at[slab], dst_ref=landing(here),
            send_sem=all_sent.at[0], recv_sem=row_recv.at[nearest],
            device_id=device(slab), device_id_type=MESH,
        )
        tags = pltpu.make_async_remote_copy(
            src_ref=sent_values.at[slab], dst_ref=got_values.at[t],
            send_sem=all_sent.at[1], recv_sem=value_recv.at[nearest],
            device_id=device(slab), device_id_type=MESH,
        )
        return rows, tags

    keep = (
        pltpu.make_async_copy(sent.at[me], landing(here), row_recv.at[nearest]),
        pltpu.make_async_copy(sent_values.at[me], got_values.at[t], value_recv.at[nearest]),
    )

    def place(at):
        first = at * share
        wanted = lax.broadcasted_iota(jnp.int32, (block, count), 0) + first * CAP
        pick = (wanted == slot_ref[...]).astype(jnp.float32).astype(jnp.bfloat16)
        rows = jnp.dot(pick, rows_ref[...], preferred_element_type=jnp.float32).astype(jnp.bfloat16)
        tags = lax.dot_general(
            values, pick, (((1,), (1,)), ((), ())), preferred_element_type=jnp.float32
        )[:1]
        for inner in range(share):
            sent[first + inner] = rows[inner * CAP : (inner + 1) * CAP]
            sent_values[first + inner, :, :CAP] = tags[:, inner * CAP : (inner + 1) * CAP]

    column_blocks = planes * row_devs // share
    depth = t // 4

    def order(turn):
        column = turn // column_blocks
        along = jnp.where(column & 1 == 1, depth, planes - 1 - depth)
        own = along * row_devs // share
        return column * column_blocks + (own ^ lax.rem(turn, column_blocks)), along

    def send(turn):
        at, along = order(turn)
        key = lax.rem(along * row_devs, share) + r
        for inner in range(share):
            slab = at * share + (key ^ inner)

            @pl.when(slab != me)
            def _():
                rows, tags = copies(slab)
                rows.start()

                @pl.when(r == 0)
                def _():
                    tags.start()

            @pl.when(slab == me)
            def _():
                keep[0].start()

                @pl.when(r == 0)
                def _():
                    keep[1].start()

    rows_in.wait()
    place(order(0)[0])
    pl.semaphore_wait(barrier, slabs - 1)
    send(0)

    def step(turn, _):
        place(order(turn)[0])
        send(turn)
        return 0

    lax.fori_loop(1, blocks, step, 0)

    fetch.wait()

    def divide(k, _):
        rows = pl.ds(pl.multiple_of(k * LANES, LANES), LANES)
        high = dynamics[rows, :].astype(jnp.bfloat16)
        dyn_high[rows, :] = high
        return 0

    lax.fori_loop(0, subs, divide, 0)
    gain[...] = jnp.zeros_like(gain)
    moment[...] = jnp.zeros_like(moment)

    def gather(turn, _):
        at = visit(nearest, turn, groups)
        own = pl.ds(pl.multiple_of(at * block, block), block)
        named = pl.ds(at * chips, chips)
        pltpu.make_async_copy(got.at[own], got.at[own], row_recv.at[at]).wait()
        pltpu.make_async_copy(got_values.at[named], got_values.at[named], value_recv.at[at]).wait()
        rows = got[own, :]
        turned[...] = rows.T
        tags = jnp.concatenate(
            [got_values[at * chips + k][:, :CAP] for k in range(chips)], axis=1
        )
        tags = jnp.broadcast_to(tags, (8, block)).astype(jnp.bfloat16)
        moment[...] += jnp.dot(tags, rows, preferred_element_type=jnp.float32)

        def column(k, _):
            cols = pl.ds(pl.multiple_of(k * wide, wide), wide)
            gain[:, cols] += jnp.dot(turned[...], got[own, cols], preferred_element_type=jnp.float32)
            return 0

        lax.fori_loop(0, width // wide, column, 0)
        return 0

    lax.fori_loop(0, groups, gather, 0)

    def push(source, target, send_sem, recv_sem, peer):
        return pltpu.make_async_remote_copy(
            src_ref=source, dst_ref=target, send_sem=send_sem, recv_sem=recv_sem,
            device_id=peer, device_id_type=MESH,
        )

    lend = push(b_ref, b_got, lend_sem.at[0], lend_sem.at[1], partner)

    def columns(k):
        return pl.ds(pl.multiple_of(k * tile, tile), tile)

    def part(i, k):
        cols = columns(k)
        source = right if i else halves
        return push(
            source.at[i, :, cols], right.at[i, :, cols], tile_send,
            tile_recv.at[i, k if i else k // 2], partner,
        )

    for sub in range(subs):
        b_ref[sub : sub + 1, :] = sigma_gain * moment[:1, sub * LANES : (sub + 1) * LANES]

    for k in range(tiles):
        rows = slice(k * tile, (k + 1) * tile)
        rounded[rows, :] = gain[rows, :].astype(jnp.bfloat16)

    def span(k):
        return pl.ds(pl.multiple_of(k * wide, wide), wide)

    spans = width // wide

    def give(k):
        cols = span(k)
        return push(
            halves.at[0, :, cols], right.at[0, :, cols], tile_send, tile_recv.at[0, k], partner
        )

    def settle(cols):
        moved = jnp.dot(rounded[...], dyn_high[:, cols], preferred_element_type=jnp.float32)
        change = dynamics[:, cols] - sigma_gain * (gain[:, cols] + moved)
        gain[:, cols] = change
        high = change.astype(jnp.bfloat16)
        halves[0, :, cols] = high
        halves[1, :, cols] = (change - high.astype(jnp.float32)).astype(jnp.bfloat16)

    @pl.when(r == 0)
    def _():
        lend.start()

        def settle_sent(k, _):
            settle(columns(k))
            part(0, k).start()
            return 0

        lax.fori_loop(0, tiles, settle_sent, 0)

    @pl.when(r == 1)
    def _():
        def settle_kept(k, _):
            settle(span(k))
            give(k).start()
            return 0

        lax.fori_loop(0, spans, settle_kept, 0)

    lane = lax.broadcasted_iota(jnp.int32, (subs, LANES), 1)
    line = lax.broadcasted_iota(jnp.int32, (subs, LANES), 0)
    group = LANES

    def apply(matrix, vector):
        pieces = [jnp.broadcast_to(vector[k : k + 1, :], (subs, LANES)) for k in range(subs)]

        def rows(step, total):
            for inner in range(group):
                g = step * group + inner
                own = pl.ds(pl.multiple_of(g * subs, subs), subs)
                part = matrix[own, 0:LANES] * pieces[0]
                for k in range(1, subs):
                    part = part + matrix[own, k * LANES : (k + 1) * LANES] * pieces[k]
                total = jnp.where(lane == g, jnp.sum(part, axis=1, keepdims=True), total)
            return total

        total = lax.fori_loop(0, LANES // group, rows, jnp.zeros((subs, LANES), jnp.float32))
        result = jnp.zeros((subs, LANES), jnp.float32)
        for k in range(subs):
            spots = lane // subs + k * (LANES // subs)
            moved = jnp.take_along_axis(total, spots, axis=1)
            kept = jnp.where(line == lax.rem(lane, subs), moved, 0.0)
            result = jnp.where(line == k, jnp.sum(kept, axis=0, keepdims=True), result)
        return result

    @pl.when(r == 0)
    def _():
        def refine(j, cols):
            deep = span(j)
            return jnp.dot(
                right[0, :, deep], halves[1, deep, cols], preferred_element_type=jnp.float32
            )

        for j in range(spans - 1):
            give(j).wait_recv()

            def early(k, _):
                cols = span(k)
                known = halves[1, :, cols].astype(jnp.float32) if j == 0 else whole[:, cols]
                whole[:, cols] = known + refine(j, cols)
                return 0

            lax.fori_loop(0, spans, early, 0)

        give(spans - 1).wait_recv()

        def late(k, _):
            cols = columns(k)
            right[1, :, cols] = (whole[:, cols] + refine(spans - 1, cols)).astype(jnp.bfloat16)
            part(1, k).start()
            return 0

        lax.fori_loop(0, tiles, late, 0)
        lend.wait_send()
        push(halves, right, tile_send, tile_recv.at[0, 0], partner).wait_send()

    @pl.when(r == 1)
    def _():
        lend.wait_recv()
        b_ref[...] += b_got[...] + apply(gain, b_got[...])
        def compose_high(k, _):
            cols = span(k)
            pltpu.make_async_copy(
                right.at[0, :, cols], right.at[0, :, cols], tile_recv.at[0, k]
            ).wait()
            high = right[0, :, cols]
            whole[:, cols] = (
                gain[:, cols] + high.astype(jnp.float32)
                + jnp.dot(halves[0], high, preferred_element_type=jnp.float32)
                + jnp.dot(halves[1], high, preferred_element_type=jnp.float32)
            )
            return 0

        lax.fori_loop(0, spans, compose_high, 0)

        def compose_low(k, _):
            cols = columns(k)
            part(1, k).wait_recv()
            whole[:, cols] += right[1, :, cols].astype(jnp.float32)
            return 0

        lax.fori_loop(0, tiles, compose_low, 0)
        push(halves.at[0], right.at[0], tile_send, tile_recv.at[0, 0], partner).wait_send()

    onward = push(went, came, pass_send.at[1], pass_recv.at[0], (after, 1))
    aside = push(went, came, pass_send.at[0], pass_recv.at[0], (after, 0))

    @pl.when(place_here == 0)
    def _():
        came[...] = start_ref[...]

    @pl.when(place_here > 0)
    def _():
        onward.wait_recv()

    passing = (r == 1) & (place_here < last)

    @pl.when(r == 1)
    def _():
        state = came[...]
        went[...] = apply(whole, state) + (b_ref[...] + state)

    @pl.when(passing)
    def _():
        onward.start()
        aside.start()

    @pl.when(r == 0)
    def _():
        state = came[...]
        went[...] = apply(gain, state) + (b_ref[...] + state)

    stays = place_here == t

    def report(core, sender):
        return push(
            went, back.at[sender], out_send.at[core], out_recv.at[sender], (place_here, core)
        )

    for core in range(2):
        @pl.when(jnp.logical_not(stays & (r == core)))
        def _():
            report(core, r).start()

        @pl.when(stays & (r == core))
        def _():
            back[core] = went[...]

    for core in range(2):
        @pl.when(jnp.logical_not(stays & (r == core)))
        def _():
            report(core, core).wait_recv()
            report(core, r).wait_send()

    part = subs // 2

    @pl.when(r == 0)
    def _():
        out_ref[0] = back[0, :part, :]
        out_ref[1] = back[1, :part, :]

    @pl.when(r == 1)
    def _():
        out_ref[0] = back[0, part:, :]
        out_ref[1] = back[1, part:, :]

    @pl.when(passing)
    def _():
        onward.wait_send()
        aside.wait_send()

    pltpu.make_async_copy(
        sent.at[pl.ds(0, slabs - 1)], sent.at[pl.ds(0, slabs - 1)], all_sent.at[0]
    ).wait()

    @pl.when(r == 0)
    def _():
        pltpu.make_async_copy(
            sent_values.at[pl.ds(0, slabs - 1)], sent_values.at[pl.ds(0, slabs - 1)], all_sent.at[1]
        ).wait()


def body(initial, dynamics, obs_rows, obs_values, obs_slab):
    time_devs = lax.axis_size("tm")
    row_devs = lax.axis_size("row")
    width = dynamics.shape[1]
    count, local = obs_rows.shape
    slabs = time_devs * row_devs
    subs = width // LANES
    tiles = width // 256
    vmem = pl.BlockSpec(memory_space=pltpu.VMEM)
    anywhere = pl.BlockSpec(memory_space=pl.ANY)
    small = pltpu.VMEM((subs, LANES), jnp.float32)
    square = pltpu.VMEM((width, width), jnp.float32)
    halves = pltpu.VMEM((2, width, width), jnp.bfloat16)
    sems = pltpu.SemaphoreType.DMA((time_devs * CAP // 256,))
    states = pl.pallas_call(
        observer_kernel,
        out_shape=jax.ShapeDtypeStruct((2, subs // 2, LANES), jnp.float32),
        in_specs=[vmem, anywhere, vmem, anywhere, vmem],
        out_specs=vmem,
        scratch_shapes=[
            pltpu.VMEM((count, local), jnp.bfloat16),
            pltpu.VMEM((1, count), jnp.float32),
            pltpu.VMEM((slabs, CAP, local), jnp.bfloat16),
            pltpu.VMEM((slabs, 1, LANES), jnp.float32),
            pltpu.VMEM((1, count), jnp.int32),
            pltpu.VMEM((time_devs * CAP, width), jnp.bfloat16),
            pltpu.VMEM((time_devs, 1, LANES), jnp.float32),
            square,
            pltpu.VMEM((width, width), jnp.bfloat16),
            pltpu.VMEM((width, 256), jnp.bfloat16),
            pltpu.VMEM((width, width), jnp.bfloat16),
            square,
            pltpu.VMEM((8, width), jnp.float32),
            square,
            halves,
            halves,
            small,
            small,
            small,
            small,
            pltpu.VMEM((2, subs, LANES), jnp.float32),
            pltpu.SemaphoreType.DMA((2,)),
            sems,
            sems,
            pltpu.SemaphoreType.DMA((2,)),
            pltpu.SemaphoreType.DMA((2,)),
            pltpu.SemaphoreType.DMA,
            pltpu.SemaphoreType.DMA((2, tiles)),
            pltpu.SemaphoreType.DMA((2,)),
            pltpu.SemaphoreType.DMA((1,)),
            pltpu.SemaphoreType.DMA((2,)),
            pltpu.SemaphoreType.DMA((2,)),
        ],
        compiler_params=pltpu.CompilerParams(
            collective_id=0, has_side_effects=True, vmem_limit_bytes=60 << 20
        ),
        name="observer",
    )(
        obs_slab.reshape(1, -1),
        obs_rows,
        obs_values.reshape(-1, LANES),
        dynamics,
        initial.reshape(subs, LANES),
    )
    return states.reshape(2, width // 2)


def solution(mesh):
    placed = (P(), P(), P("tm", "row"), P("tm"), P("tm", None))
    return jax.shard_map(
        body, mesh=mesh, in_specs=placed, out_specs=P("tm", "row"), check_vma=False
    )
```

```python
import jax
import jax.numpy as jnp
from jax import lax
from jax.experimental import pallas as pl
from jax.experimental.pallas import tpu as pltpu
from jax.sharding import PartitionSpec as P

CAP = 64
LANES = 128
MESH = pl.DeviceIdType.MESH

sigma_gain = 0.3


def visit(own, turn, total):
    if total & (total - 1):
        return lax.rem(own + turn, total)
    return own ^ turn


def chip_at(place, planes):
    column = place // planes
    depth = lax.rem(place, planes)
    depth = jnp.where(column & 1 == 1, depth, planes - 1 - depth)
    turn = (column + 3) & 3
    return depth * 4 + (turn ^ (turn >> 1))


def place_of(chip, planes):
    depth, turn = chip // 4, chip & 3
    column = ((turn ^ (turn >> 1)) + 1) & 3
    depth = jnp.where(column & 1 == 1, depth, planes - 1 - depth)
    return column * planes + depth


def observer_kernel(
    target_ref, rows_hbm, values_ref, dynamics_ref, start_ref, out_ref,
    rows_ref, values_row, sent, sent_values, slot_ref, got, got_values, dynamics, dyn_high, turned, rounded, gain, moment,
    whole, halves, right, b_ref, b_got, came, went, back,
    all_sent, row_recv, value_recv, own_sem, lend_sem, tile_send, tile_recv, pass_send, pass_recv,
    out_send, out_recv,
):
    time_devs, row_devs = lax.axis_size("tm"), lax.axis_size("row")
    t, r = lax.axis_index("tm"), lax.axis_index("row")
    slabs = time_devs * row_devs
    last = time_devs - 1
    planes = time_devs // 4
    place_here = place_of(t, planes)
    after = chip_at(jnp.minimum(place_here + 1, last), planes)
    me = place_here * row_devs + r
    here = t * row_devs + r
    partner = (t, 1 - r)
    count, local = rows_ref.shape
    width = local * row_devs
    subs = width // LANES
    tile = 256
    tiles = width // tile
    wide = 2 * tile
    block = 256
    share = block // CAP
    blocks = slabs // share

    def device(slab):
        return (chip_at(slab // row_devs, planes), lax.rem(slab, row_devs))

    barrier = pltpu.get_barrier_semaphore()

    def greet(turn, _):
        other = visit(here, slabs - 1 - turn, slabs)
        pl.semaphore_signal(
            barrier, inc=1, device_id=(other // row_devs, lax.rem(other, row_devs)),
            device_id_type=MESH,
        )
        return 0

    lax.fori_loop(0, slabs - 1, greet, 0)
    rows_in = pltpu.make_async_copy(rows_hbm, rows_ref, own_sem.at[1])
    rows_in.start()
    fetch = pltpu.make_async_copy(dynamics_ref, dynamics, own_sem.at[0])
    fetch.start()

    before = (
        lax.broadcasted_iota(jnp.int32, (block, block), 0)
        < lax.broadcasted_iota(jnp.int32, (block, block), 1)
    ).astype(jnp.float32).astype(jnp.bfloat16)
    slab_of = lax.broadcasted_iota(jnp.int32, (slabs, block), 0)
    carry = (slab_of[:, :1] * CAP).astype(jnp.float32)
    for start in range(0, count, block):
        named = (target_ref[:, start : start + block] == slab_of).astype(jnp.float32)
        ahead = jnp.dot(named.astype(jnp.bfloat16), before, preferred_element_type=jnp.float32)
        slot = jnp.sum(named * (ahead + carry), axis=0, keepdims=True)
        slot_ref[:, start : start + block] = slot.astype(jnp.int32)
        carry = carry + jnp.sum(named, axis=1, keepdims=True)

    spread = values_ref[...].astype(jnp.float32)
    for line in range(count // LANES):
        values_row[:, line * LANES : (line + 1) * LANES] = spread[line : line + 1, :]
    values = jnp.broadcast_to(values_row[...], (8, count)).astype(jnp.bfloat16)
    sent_values[...] = jnp.zeros_like(sent_values)

    def landing(source):
        rows = pl.ds(pl.multiple_of(source // row_devs * CAP, CAP), CAP)
        cols = pl.ds(pl.multiple_of(lax.rem(source, row_devs) * local, local), local)
        return got.at[rows, cols]

    chips = block // CAP
    groups = time_devs // chips
    nearest = t // chips

    def copies(slab):
        rows = pltpu.make_async_remote_copy(
            src_ref=sent.at[slab], dst_ref=landing(here),
            send_sem=all_sent.at[0], recv_sem=row_recv.at[nearest],
            device_id=device(slab), device_id_type=MESH,
        )
        tags = pltpu.make_async_remote_copy(
            src_ref=sent_values.at[slab], dst_ref=got_values.at[t],
            send_sem=all_sent.at[1], recv_sem=value_recv.at[nearest],
            device_id=device(slab), device_id_type=MESH,
        )
        return rows, tags

    keep = (
        pltpu.make_async_copy(sent.at[me], landing(here), row_recv.at[nearest]),
        pltpu.make_async_copy(sent_values.at[me], got_values.at[t], value_recv.at[nearest]),
    )

    def place(at):
        first = at * share
        wanted = lax.broadcasted_iota(jnp.int32, (block, count), 0) + first * CAP
        pick = (wanted == slot_ref[...]).astype(jnp.float32).astype(jnp.bfloat16)
        rows = jnp.dot(pick, rows_ref[...], preferred_element_type=jnp.float32).astype(jnp.bfloat16)
        tags = lax.dot_general(
            values, pick, (((1,), (1,)), ((), ())), preferred_element_type=jnp.float32
        )[:1]
        for inner in range(share):
            sent[first + inner] = rows[inner * CAP : (inner + 1) * CAP]
            sent_values[first + inner, :, :CAP] = tags[:, inner * CAP : (inner + 1) * CAP]

    column_blocks = planes * row_devs // share
    depth = t // 4

    def order(turn):
        column = turn // column_blocks
        along = jnp.where(column & 1 == 1, depth, planes - 1 - depth)
        own = along * row_devs // share
        return column * column_blocks + (own ^ lax.rem(turn, column_blocks)), along

    def send(turn):
        at, along = order(turn)
        key = lax.rem(along * row_devs, share) + r
        for inner in range(share):
            slab = at * share + (key ^ inner)

            @pl.when(slab != me)
            def _():
                rows, tags = copies(slab)
                rows.start()

                @pl.when(r == 0)
                def _():
                    tags.start()

            @pl.when(slab == me)
            def _():
                keep[0].start()

                @pl.when(r == 0)
                def _():
                    keep[1].start()

    rows_in.wait()
    place(order(0)[0])
    pl.semaphore_wait(barrier, slabs - 1)
    send(0)

    def step(turn, _):
        place(order(turn)[0])
        send(turn)
        return 0

    lax.fori_loop(1, blocks, step, 0)

    fetch.wait()

    def divide(k, _):
        rows = pl.ds(pl.multiple_of(k * LANES, LANES), LANES)
        high = dynamics[rows, :].astype(jnp.bfloat16)
        dyn_high[rows, :] = high
        return 0

    lax.fori_loop(0, subs, divide, 0)
    gain[...] = jnp.zeros_like(gain)
    moment[...] = jnp.zeros_like(moment)

    def gather(turn, _):
        at = visit(nearest, turn, groups)
        own = pl.ds(pl.multiple_of(at * block, block), block)
        named = pl.ds(at * chips, chips)
        pltpu.make_async_copy(got.at[own], got.at[own], row_recv.at[at]).wait()
        pltpu.make_async_copy(got_values.at[named], got_values.at[named], value_recv.at[at]).wait()
        rows = got[own, :]
        turned[...] = rows.T
        tags = jnp.concatenate(
            [got_values[at * chips + k][:, :CAP] for k in range(chips)], axis=1
        )
        tags = jnp.broadcast_to(tags, (8, block)).astype(jnp.bfloat16)
        moment[...] += jnp.dot(tags, rows, preferred_element_type=jnp.float32)

        def column(k, _):
            cols = pl.ds(pl.multiple_of(k * wide, wide), wide)
            gain[:, cols] += jnp.dot(turned[...], got[own, cols], preferred_element_type=jnp.float32)
            return 0

        lax.fori_loop(0, width // wide, column, 0)
        return 0

    lax.fori_loop(0, groups, gather, 0)

    def push(source, target, send_sem, recv_sem, peer):
        return pltpu.make_async_remote_copy(
            src_ref=source, dst_ref=target, send_sem=send_sem, recv_sem=recv_sem,
            device_id=peer, device_id_type=MESH,
        )

    lend = push(b_ref, b_got, lend_sem.at[0], lend_sem.at[1], partner)

    def columns(k):
        return pl.ds(pl.multiple_of(k * tile, tile), tile)

    def part(i, k):
        cols = columns(k)
        source = right if i else halves
        return push(
            source.at[i, :, cols], right.at[i, :, cols], tile_send,
            tile_recv.at[i, k if i else k // 2], partner,
        )

    for sub in range(subs):
        b_ref[sub : sub + 1, :] = sigma_gain * moment[:1, sub * LANES : (sub + 1) * LANES]

    for k in range(tiles):
        rows = slice(k * tile, (k + 1) * tile)
        rounded[rows, :] = gain[rows, :].astype(jnp.bfloat16)

    def span(k):
        return pl.ds(pl.multiple_of(k * wide, wide), wide)

    spans = width // wide

    def give(k):
        cols = span(k)
        return push(
            halves.at[0, :, cols], right.at[0, :, cols], tile_send, tile_recv.at[0, k], partner
        )

    def settle(cols):
        moved = jnp.dot(rounded[...], dyn_high[:, cols], preferred_element_type=jnp.float32)
        change = dynamics[:, cols] - sigma_gain * (gain[:, cols] + moved)
        gain[:, cols] = change
        high = change.astype(jnp.bfloat16)
        halves[0, :, cols] = high
        halves[1, :, cols] = (change - high.astype(jnp.float32)).astype(jnp.bfloat16)

    @pl.when(r == 0)
    def _():
        lend.start()

        def settle_sent(k, _):
            settle(span(k))
            for inner in range(wide // tile):
                part(0, k * (wide // tile) + inner).start()
            return 0

        lax.fori_loop(0, spans, settle_sent, 0)

    @pl.when(r == 1)
    def _():
        def settle_kept(k, _):
            settle(span(k))
            give(k).start()
            return 0

        lax.fori_loop(0, spans, settle_kept, 0)

    lane = lax.broadcasted_iota(jnp.int32, (subs, LANES), 1)
    line = lax.broadcasted_iota(jnp.int32, (subs, LANES), 0)
    group = LANES

    def apply(matrix, vector):
        pieces = [jnp.broadcast_to(vector[k : k + 1, :], (subs, LANES)) for k in range(subs)]

        def rows(step, total):
            for inner in range(group):
                g = step * group + inner
                own = pl.ds(pl.multiple_of(g * subs, subs), subs)
                part = matrix[own, 0:LANES] * pieces[0]
                for k in range(1, subs):
                    part = part + matrix[own, k * LANES : (k + 1) * LANES] * pieces[k]
                total = jnp.where(lane == g, jnp.sum(part, axis=1, keepdims=True), total)
            return total

        total = lax.fori_loop(0, LANES // group, rows, jnp.zeros((subs, LANES), jnp.float32))
        result = jnp.zeros((subs, LANES), jnp.float32)
        for k in range(subs):
            spots = lane // subs + k * (LANES // subs)
            moved = jnp.take_along_axis(total, spots, axis=1)
            kept = jnp.where(line == lax.rem(lane, subs), moved, 0.0)
            result = jnp.where(line == k, jnp.sum(kept, axis=0, keepdims=True), result)
        return result

    @pl.when(r == 0)
    def _():
        def refine(j, cols):
            deep = span(j)
            return jnp.dot(
                right[0, :, deep], halves[1, deep, cols], preferred_element_type=jnp.float32
            )

        for j in range(spans - 1):
            give(j).wait_recv()

            def early(k, _):
                cols = span(k)
                known = halves[1, :, cols].astype(jnp.float32) if j == 0 else whole[:, cols]
                whole[:, cols] = known + refine(j, cols)
                return 0

            lax.fori_loop(0, spans, early, 0)

        give(spans - 1).wait_recv()

        def late(k, _):
            cols = columns(k)
            right[1, :, cols] = (whole[:, cols] + refine(spans - 1, cols)).astype(jnp.bfloat16)
            part(1, k).start()
            return 0

        lax.fori_loop(0, tiles, late, 0)
        lend.wait_send()
        push(halves, right, tile_send, tile_recv.at[0, 0], partner).wait_send()

    @pl.when(r == 1)
    def _():
        lend.wait_recv()
        b_ref[...] += b_got[...] + apply(gain, b_got[...])
        def compose_high(k, _):
            cols = span(k)
            pltpu.make_async_copy(
                right.at[0, :, cols], right.at[0, :, cols], tile_recv.at[0, k]
            ).wait()
            high = right[0, :, cols]
            whole[:, cols] = (
                gain[:, cols] + high.astype(jnp.float32)
                + jnp.dot(halves[0], high, preferred_element_type=jnp.float32)
                + jnp.dot(halves[1], high, preferred_element_type=jnp.float32)
            )
            return 0

        lax.fori_loop(0, spans, compose_high, 0)

        def compose_low(k, _):
            cols = columns(k)
            part(1, k).wait_recv()
            whole[:, cols] += right[1, :, cols].astype(jnp.float32)
            return 0

        lax.fori_loop(0, tiles, compose_low, 0)
        push(halves.at[0], right.at[0], tile_send, tile_recv.at[0, 0], partner).wait_send()

    onward = push(went, came, pass_send.at[1], pass_recv.at[0], (after, 1))
    aside = push(went, came, pass_send.at[0], pass_recv.at[0], (after, 0))

    @pl.when(place_here == 0)
    def _():
        came[...] = start_ref[...]

    @pl.when(place_here > 0)
    def _():
        onward.wait_recv()

    passing = (r == 1) & (place_here < last)

    @pl.when(r == 1)
    def _():
        state = came[...]
        went[...] = apply(whole, state) + (b_ref[...] + state)

    @pl.when(passing)
    def _():
        onward.start()
        aside.start()

    @pl.when(r == 0)
    def _():
        state = came[...]
        went[...] = apply(gain, state) + (b_ref[...] + state)

    stays = place_here == t

    def report(core, sender):
        return push(
            went, back.at[sender], out_send.at[core], out_recv.at[sender], (place_here, core)
        )

    for core in range(2):
        @pl.when(jnp.logical_not(stays & (r == core)))
        def _():
            report(core, r).start()

        @pl.when(stays & (r == core))
        def _():
            back[core] = went[...]

    for core in range(2):
        @pl.when(jnp.logical_not(stays & (r == core)))
        def _():
            report(core, core).wait_recv()
            report(core, r).wait_send()

    part = subs // 2

    @pl.when(r == 0)
    def _():
        out_ref[0] = back[0, :part, :]
        out_ref[1] = back[1, :part, :]

    @pl.when(r == 1)
    def _():
        out_ref[0] = back[0, part:, :]
        out_ref[1] = back[1, part:, :]

    @pl.when(passing)
    def _():
        onward.wait_send()
        aside.wait_send()

    pltpu.make_async_copy(
        sent.at[pl.ds(0, slabs - 1)], sent.at[pl.ds(0, slabs - 1)], all_sent.at[0]
    ).wait()

    @pl.when(r == 0)
    def _():
        pltpu.make_async_copy(
            sent_values.at[pl.ds(0, slabs - 1)], sent_values.at[pl.ds(0, slabs - 1)], all_sent.at[1]
        ).wait()


def body(initial, dynamics, obs_rows, obs_values, obs_slab):
    time_devs = lax.axis_size("tm")
    row_devs = lax.axis_size("row")
    width = dynamics.shape[1]
    count, local = obs_rows.shape
    slabs = time_devs * row_devs
    subs = width // LANES
    tiles = width // 256
    vmem = pl.BlockSpec(memory_space=pltpu.VMEM)
    anywhere = pl.BlockSpec(memory_space=pl.ANY)
    small = pltpu.VMEM((subs, LANES), jnp.float32)
    square = pltpu.VMEM((width, width), jnp.float32)
    halves = pltpu.VMEM((2, width, width), jnp.bfloat16)
    sems = pltpu.SemaphoreType.DMA((time_devs * CAP // 256,))
    states = pl.pallas_call(
        observer_kernel,
        out_shape=jax.ShapeDtypeStruct((2, subs // 2, LANES), jnp.float32),
        in_specs=[vmem, anywhere, vmem, anywhere, vmem],
        out_specs=vmem,
        scratch_shapes=[
            pltpu.VMEM((count, local), jnp.bfloat16),
            pltpu.VMEM((1, count), jnp.float32),
            pltpu.VMEM((slabs, CAP, local), jnp.bfloat16),
            pltpu.VMEM((slabs, 1, LANES), jnp.float32),
            pltpu.VMEM((1, count), jnp.int32),
            pltpu.VMEM((time_devs * CAP, width), jnp.bfloat16),
            pltpu.VMEM((time_devs, 1, LANES), jnp.float32),
            square,
            pltpu.VMEM((width, width), jnp.bfloat16),
            pltpu.VMEM((width, 256), jnp.bfloat16),
            pltpu.VMEM((width, width), jnp.bfloat16),
            square,
            pltpu.VMEM((8, width), jnp.float32),
            square,
            halves,
            halves,
            small,
            small,
            small,
            small,
            pltpu.VMEM((2, subs, LANES), jnp.float32),
            pltpu.SemaphoreType.DMA((2,)),
            sems,
            sems,
            pltpu.SemaphoreType.DMA((2,)),
            pltpu.SemaphoreType.DMA((2,)),
            pltpu.SemaphoreType.DMA,
            pltpu.SemaphoreType.DMA((2, tiles)),
            pltpu.SemaphoreType.DMA((2,)),
            pltpu.SemaphoreType.DMA((1,)),
            pltpu.SemaphoreType.DMA((2,)),
            pltpu.SemaphoreType.DMA((2,)),
        ],
        compiler_params=pltpu.CompilerParams(
            collective_id=0, has_side_effects=True, vmem_limit_bytes=60 << 20
        ),
        name="observer",
    )(
        obs_slab.reshape(1, -1),
        obs_rows,
        obs_values.reshape(-1, LANES),
        dynamics,
        initial.reshape(subs, LANES),
    )
    return states.reshape(2, width // 2)


def solution(mesh):
    placed = (P(), P(), P("tm", "row"), P("tm"), P("tm", None))
    return jax.shard_map(
        body, mesh=mesh, in_specs=placed, out_specs=P("tm", "row"), check_vma=False
    )
```
